128 devices in a mesh: section: 2 (over y_hi), row: 8 (over z, core), tp: 8 (over x, y_lo).
Axes of the slice: x: 4, y: 4 (y_hi: 2, y_lo: 2; y = y_hi * 2 + y_lo), z: 4, core: 2. Of those that a mesh axis runs over, the one named last changes fastest.
Arguments:
- section_feeds: bfloat16 [2, 2, 128, 8192], P('section', None, None, 'row'), may hold values from -6 to 6
- norm_gain: float32 [2, 8192], P('section', 'row'), may hold values from 0.1 to 1.9
- up_weight: bfloat16 [2, 8192, 32768], P('section', 'row', 'tp'), may hold values from -0.0625 to 0.0625
- down_weight: bfloat16 [2, 32768, 8192], P('section', 'tp', 'row'), may hold values from -0.03125 to 0.03125
Outputs:
- section_ends: bfloat16 [2, 2, 128, 8192], P('section', None, None, 'row')
The draws below stay inside these ranges and needn't reach their ends.
All inputs are finite; a program needn't handle non-finite values.
Results may differ from the reference program's by a relative error of at most 0.011.
Values may be sent and summed in bfloat16 or wider, within the bound.
No kernel may reach another device: no remote copies, remote signals or barrier semaphores. Data moves between devices by JAX's collectives and lax.ppermute only.
A program may use at most 128 MiB of HBM per device.

```python
import jax
import jax.numpy as jnp
from jax import lax

D = 8192
FF = 32768
TOK = 128
MICRO = 2


def block_levels(own_key, extent, split, smallest, largest):
    def one(axis_at, shards_of):
        draws = jax.random.uniform(jax.random.fold_in(jax.random.fold_in(own_key, 6), axis_at), (shards_of,), jnp.float32, smallest / len(split), largest / len(split))
        return jnp.repeat(jnp.exp(draws), extent[axis_at] // shards_of).reshape((-1,) + (1,) * (len(extent) - axis_at - 1))

    level = one(*split[0])
    for cut in split[1:]:
        level = level * one(*cut)
    return level


def gaussian(rng, extent, width, limit, split=(), dtype=jnp.bfloat16):
    loudness = block_levels(rng, extent, split, -0.22, 0.18) if split else 1.0
    values = jax.random.normal(rng, extent, jnp.float32) * width * loudness
    return jnp.minimum(jnp.maximum(values, -limit), limit).astype(dtype)


def setup_inputs(seed: int = 0) -> dict:
    seeds = jax.random.split(jax.random.key(seed), 5)
    section_feeds = gaussian(seeds[0], (2, MICRO, TOK, D), 1.0, 6.0, ((0, 2), (3, 8)))
    norm_gain = jnp.clip(1.0 + 0.18 * jax.random.normal(seeds[1], (2, D), jnp.float32), 0.1, 1.9)
    up_weight = gaussian(seeds[2], (2, D, FF), D ** -0.5, 0.0625, ((0, 2), (1, 8), (2, 8)))
    down_weight = gaussian(seeds[3], (2, FF, D), FF ** -0.5, 0.03125, ((0, 2), (1, 8), (2, 8)))
    return dict(section_feeds=section_feeds, norm_gain=norm_gain, up_weight=up_weight, down_weight=down_weight)


epsilon = 1e-05
gelu_coeff = 0.7978845608028654

def gelu_value(inputs):
    inner = gelu_coeff * (inputs + 0.044715 * inputs * inputs * inputs)
    return 0.5 * inputs * (1.0 + jnp.tanh(inner))

def gelu_slope(inputs):
    inner = gelu_coeff * (inputs + 0.044715 * inputs * inputs * inputs)
    tangent = jnp.tanh(inner)
    return 0.5 * (1.0 + tangent) + 0.5 * inputs * (1.0 - tangent * tangent) * gelu_coeff * (1.0 + 3.0 * 0.044715 * inputs * inputs)

def layer_forward(inputs, gain_row, up_matrix, down_matrix):
    values = inputs.astype(jnp.float32)
    row_mean = lax.optimization_barrier(jnp.sum(values, axis=1)) / D
    variance = lax.optimization_barrier(jnp.sum(values * values, axis=1)) / D - row_mean * row_mean
    inv_std = lax.rsqrt(variance + epsilon)
    normed = (values - row_mean[:, None]) * inv_std[:, None]
    scaled = (normed * gain_row.astype(jnp.float32)[None, :]).astype(jnp.bfloat16)
    hidden_pre = jnp.dot(scaled, up_matrix, preferred_element_type=jnp.float32)
    hidden = gelu_value(hidden_pre).astype(jnp.bfloat16)
    branch = jnp.dot(hidden, down_matrix, preferred_element_type=jnp.float32)
    return ((values + branch).astype(jnp.bfloat16), (normed, inv_std, hidden_pre))

def layer_backward(incoming, gain_row, up_matrix, down_matrix, saved):
    normed, inv_std, hidden_pre = saved
    hidden_grad = jnp.dot(incoming, down_matrix.T, preferred_element_type=jnp.float32)
    pre_grad = (hidden_grad * gelu_slope(hidden_pre)).astype(jnp.bfloat16)
    normed_grad = jnp.dot(pre_grad, up_matrix.T, preferred_element_type=jnp.float32) * gain_row.astype(jnp.float32)[None, :]
    first_mean = lax.optimization_barrier(jnp.sum(normed_grad, axis=1)) / D
    second_mean = lax.optimization_barrier(jnp.sum(normed_grad * normed, axis=1)) / D
    result = incoming.astype(jnp.float32) + inv_std[:, None] * (normed_grad - first_mean[:, None] - normed * second_mean[:, None])
    return result.astype(jnp.bfloat16)

def reference(section_feeds, norm_gain, up_weight, down_weight):
    outputs = []
    gradients = []
    for micro_index in range(MICRO):
        middle, saved_first = layer_forward(section_feeds[0, micro_index], norm_gain[0], up_weight[0], down_weight[0])
        final, saved_second = layer_forward(middle, norm_gain[1], up_weight[1], down_weight[1])
        back_grad = layer_backward(section_feeds[1, micro_index], norm_gain[1], up_weight[1], down_weight[1], saved_second)
        gradients.append(layer_backward(back_grad, norm_gain[0], up_weight[0], down_weight[0], saved_first))
        outputs.append(final)
    return jnp.stack([jnp.stack(gradients), jnp.stack(outputs)])
```

```python
import jax
import jax.numpy as jnp
from jax import lax
from jax.sharding import PartitionSpec as P

epsilon = 1e-05
gelu_coeff = 0.7978845608028654
LANES = 128
f32 = jnp.float32
bf16 = jnp.bfloat16


def gelu_parts(inputs):
    inner = gelu_coeff * (inputs + 0.044715 * inputs * inputs * inputs)
    return jnp.tanh(inner)


def gelu_value(inputs):
    return 0.5 * inputs * (1.0 + gelu_parts(inputs))


def gelu_slope(inputs):
    tangent = gelu_parts(inputs)
    return 0.5 * (1.0 + tangent) + 0.5 * inputs * (1.0 - tangent * tangent) * gelu_coeff * (
        1.0 + 3.0 * 0.044715 * inputs * inputs
    )


def pieces(value):
    high = value.astype(bf16)
    rest = value - high.astype(f32)
    middle = rest.astype(bf16)
    low = (rest - middle.astype(f32)).astype(bf16)
    return high, middle, low


def permuted(array, axis, mapping):
    return lax.ppermute(array, axis, [(i, mapping(i)) for i in range(lax.axis_size(axis))])


def pick(array, index):
    return lax.dynamic_index_in_dim(array, index, 0, keepdims=False)


def body(section_feeds, norm_gain, up_weight, down_weight):
    up = up_weight[0]
    down = down_weight[0]
    gain = norm_gain[0]
    width, hidden = up.shape
    micro, rows = section_feeds.shape[1], section_feeds.shape[2]
    rsize, tsize = lax.axis_size("row"), lax.axis_size("tp")
    chips = rsize // 2
    total_width = width * rsize
    tokens = micro * rows
    block = tokens // rsize
    is_first = lax.axis_index("section") == 0
    row_at = lax.axis_index("row")
    tp_at = lax.axis_index("tp")
    core, chip = row_at % 2, row_at // 2
    lane = lax.broadcasted_iota(jnp.int32, (1, LANES), 1)

    def to_local(array):
        blocks = array.reshape(2, chips, block, width)
        blocks = jnp.where(core == 0, blocks, blocks[::-1])[:, ::-1]
        twice = jnp.concatenate([blocks, blocks], axis=1)
        return lax.dynamic_slice_in_dim(twice, chips - 1 - chip, chips, axis=1).reshape(
            2 * chips, block, width
        )

    def to_global(array):
        blocks = array.reshape(2, chips, block, width)[:, ::-1]
        twice = jnp.concatenate([blocks, blocks], axis=1)
        blocks = lax.dynamic_slice_in_dim(twice, chips - 1 - chip, chips, axis=1)
        return jnp.where(core == 0, blocks, blocks[::-1]).reshape(micro, rows, width)

    def hop(distance):
        return lambda i: (i + 2 * distance) % rsize

    def row_reduce(part):
        part = part.reshape(2, chips, block, part.shape[-1])
        arrived = permuted(part[1], "row", lambda i: i ^ 1)
        chip_sum = part[0].astype(f32) + arrived.astype(f32)
        sent = chip_sum.astype(bf16)
        total = chip_sum[0]
        for distance in range(1, chips):
            total = total + permuted(sent[chips - distance], "row", hop(distance)).astype(f32)
        return total

    def row_gather(chunk):
        half = jnp.stack(
            [chunk] + [permuted(chunk, "row", hop(distance)) for distance in range(1, chips)]
        )
        other = permuted(half, "row", lambda i: i ^ 1)
        return jnp.concatenate([half, other]).reshape(tokens, chunk.shape[-1])

    def tp_reduce(part):
        part = part.reshape(tsize, tokens // tsize, part.shape[-1])
        return jnp.sum(lax.all_to_all(part, "tp", 0, 0).astype(f32), axis=0)

    def tp_gather(piece):
        return lax.all_to_all(
            jnp.broadcast_to(piece[None], (tsize,) + piece.shape), "tp", 0, 0
        )

    def spread(values):
        out = jnp.zeros((values[0][0].shape[0], LANES), f32)
        for at, value in values:
            out = out + jnp.where(lane == at, value.astype(f32)[:, None], 0.0)
        return out.astype(bf16)

    def up_stats(values):
        mean = jnp.sum(values, axis=1) / width
        centred = values - mean[:, None]
        spread_sq = jnp.sum(centred * centred, axis=1)
        ext = jnp.zeros((tokens, LANES), f32)
        for at, value in enumerate(pieces(mean) + pieces(spread_sq)):
            ext = ext + jnp.where(lane == at * rsize + row_at, value.astype(f32)[:, None], 0.0)
        return (centred * gain[None, :]).astype(bf16), ext.astype(bf16)

    def with_stats(summed):
        body_part, ext = summed[:, :hidden], summed[:, hidden:]
        means = ext[:, :rsize] + ext[:, rsize : 2 * rsize] + ext[:, 2 * rsize : 3 * rsize]
        squares = (
            ext[:, 3 * rsize : 4 * rsize]
            + ext[:, 4 * rsize : 5 * rsize]
            + ext[:, 5 * rsize : 6 * rsize]
        )
        mean = jnp.sum(means, axis=1, keepdims=True) / rsize
        shift = means - mean
        variance = jnp.sum(squares + width * shift * shift, axis=1, keepdims=True) / total_width
        inv_std = lax.rsqrt(variance + epsilon)
        fixed = body_part
        for at in range(rsize):
            fixed = fixed + shift[:, at : at + 1] * gain_rows[at][None, :]
        return inv_std * fixed, mean, inv_std

    def back_ext(pre_grad, pre, mean, inv_std):
        grads = pre_grad.astype(f32)
        first = jnp.sum(grads * gain_total[None, :], axis=1, keepdims=True)
        second = jnp.sum(grads * pre, axis=1, keepdims=True)
        out = jnp.zeros((block, LANES), f32)
        at = 0
        for value in (first, second, mean / tsize, inv_std / tsize):
            for part in pieces(value):
                out = out + jnp.where(lane == at, part.astype(f32), 0.0)
                at += 1
        return out.astype(bf16)

    def back_finish(summed, incoming, inputs):
        ext = summed[:, width:]
        first, second, mean, inv_std = (
            ext[:, 3 * at : 3 * at + 1] + ext[:, 3 * at + 1 : 3 * at + 2] + ext[:, 3 * at + 2 : 3 * at + 3]
            for at in range(4)
        )
        normed = (inputs.astype(f32) - mean) * inv_std
        normed_grad = summed[:, :width] * gain[None, :]
        return incoming.astype(f32) + inv_std * (
            normed_grad - first / total_width - normed * (second / total_width)
        )

    def dot(a, b, dims):
        return lax.dot_general(a, b, (dims, ((), ())), preferred_element_type=f32)

    def up_dot(a):
        return dot(a, up, ((1,), (0,))).astype(bf16)

    def down_back_dot(a):
        return dot(a, down, ((1,), (1,))).astype(bf16)

    def down_dot(a):
        return dot(a, down, ((1,), (0,))).astype(bf16)

    def up_back_dot(a):
        return dot(a, up, ((1,), (1,))).astype(bf16)

    gain_parts = jnp.stack(pieces(gain) + (jnp.zeros((width,), bf16),) * 5)
    gain_own = jnp.sum(dot(gain_parts, up, ((1,), (0,))), axis=0)
    gain_rows = lax.all_gather(gain_own, "row")
    gain_total = jnp.sum(gain_rows, axis=0)

    feeds = to_local(section_feeds[0])
    flat = feeds.reshape(tokens, width)
    scaled, ext = up_stats(flat.astype(f32))
    part = lax.cond(is_first, lambda: up_dot(scaled), lambda: down_back_dot(flat))
    summed = row_reduce(jnp.concatenate([part, ext], axis=1))
    pre0, mean0, inv0 = with_stats(summed)
    hidden_grad1 = summed[:, :hidden]
    gathered = row_gather(gelu_value(pre0).astype(bf16))
    branch = tp_reduce(down_dot(gathered))
    own_feed = pick(feeds, tp_at)
    middle = (own_feed.astype(f32) + branch).astype(bf16)
    middle = lax.ppermute(middle, "section", [(0, 1)])
    middles = tp_gather(middle)

    scaled, ext = up_stats(middles.reshape(tokens, width).astype(f32))
    summed = row_reduce(jnp.concatenate([up_dot(scaled), ext], axis=1))
    pre1, mean1, inv1 = with_stats(summed)
    hidden1 = gelu_value(pre1).astype(bf16)
    pre_grad1 = (hidden_grad1 * gelu_slope(pre1)).astype(bf16)
    gathered = row_gather(
        jnp.concatenate([pre_grad1, back_ext(pre_grad1, pre1, mean1, inv1)], axis=1)
    )
    part = jnp.concatenate([up_back_dot(gathered[:, :hidden]), gathered[:, hidden:]], axis=1)
    back = back_finish(tp_reduce(part), own_feed, middle).astype(bf16)
    back = lax.ppermute(back, "section", [(1, 0)])
    backs = tp_gather(back)

    summed = row_reduce(down_back_dot(backs.reshape(tokens, width)))
    pre_grad0 = (summed * gelu_slope(pre0)).astype(bf16)
    chunk = jnp.where(is_first, pre_grad0, hidden1)
    gathered = row_gather(
        jnp.concatenate([chunk, back_ext(pre_grad0, pre0, mean0, inv0)], axis=1)
    )
    sides = gathered[:, :hidden]
    part = lax.cond(is_first, lambda: up_back_dot(sides), lambda: down_dot(sides))
    summed = tp_reduce(jnp.concatenate([part, gathered[:, hidden:]], axis=1))
    ends = jnp.where(
        is_first, back_finish(summed, back, own_feed), middle.astype(f32) + summed[:, :width]
    ).astype(bf16)
    return to_global(tp_gather(ends))[None]


def solution(mesh):
    placed = (
        P("section", None, None, "row"),
        P("section", "row"),
        P("section", "row", "tp"),
        P("section", "tp", "row"),
    )
    return jax.shard_map(
        body, mesh=mesh, in_specs=placed, out_specs=P("section", None, None, "row"), check_vma=False
    )
```

```python
import functools

import jax
import jax.numpy as jnp
from jax import lax
from jax.experimental import pallas as pl
from jax.experimental.pallas import tpu as pltpu
from jax.sharding import PartitionSpec as P

epsilon = 1e-05
gelu_coeff = 0.7978845608028654
LANES = 128
EXTRA = 32
f32 = jnp.float32
bf16 = jnp.bfloat16
NN = (((1,), (0,)), ((), ()))
NT = (((1,), (1,)), ((), ()))
HBM = pl.BlockSpec(memory_space=pltpu.HBM)
VMEM = pl.BlockSpec(memory_space=pltpu.VMEM)
SMEM = pl.BlockSpec(memory_space=pltpu.SMEM)


def gelu_tangent(inputs):
    return jnp.tanh(gelu_coeff * (inputs + 0.044715 * inputs * inputs * inputs))


def gelu_value(inputs):
    return 0.5 * inputs * (1.0 + gelu_tangent(inputs))


def gelu_slope(inputs):
    tangent = gelu_tangent(inputs)
    return 0.5 * (1.0 + tangent) + 0.5 * inputs * (1.0 - tangent * tangent) * gelu_coeff * (
        1.0 + 3.0 * 0.044715 * inputs * inputs
    )


def pieces(value):
    high = value.astype(bf16)
    rest = value - high.astype(f32)
    middle = rest.astype(bf16)
    low = (rest - middle.astype(f32)).astype(bf16)
    return high, middle, low


def pieces32(value):
    return tuple(part.astype(f32) for part in pieces(value))


def mul(a, b, dims):
    return lax.dot_general(a, b, dims, preferred_element_type=f32)


def norm_stats(raw, gain_row):
    values = raw.astype(f32)
    mean = jnp.sum(values, axis=1, keepdims=True) / values.shape[1]
    centred = values - mean
    squares = jnp.sum(centred * centred, axis=1, keepdims=True)
    return (centred * gain_row).astype(bf16), pieces32(mean) + pieces32(squares)


def put_stats(to, start, lanes, stats, row_at):
    lane = lax.broadcasted_iota(jnp.int32, (1, LANES), 1)
    ext = jnp.zeros((stats[0].shape[0], LANES), f32)
    for i, part in enumerate(stats):
        ext = ext + jnp.where(lane == i * 8 + row_at, part, 0.0)
    to[pl.ds(start, ext.shape[0]), pl.ds(lanes, LANES)] = ext.astype(to.dtype)


def placed(parts, row_at):
    spot = lax.broadcasted_iota(jnp.int32, (EXTRA, 1), 0)
    return sum(jnp.where(spot == 3 * row_at + j, part, 0.0) for j, part in enumerate(parts))


def store_halves(own, other, columns, result):
    half = result.shape[0] // 2
    own[pl.ds(0, half), columns] = result[:half]
    other[pl.ds(0, half), columns] = result[half:].astype(bf16)


def start_kernel(part, at, x, gain, up, down, *refs):
    outs, (xs_out, x_here, up_tiles, down_tiles, sems) = refs[:4], refs[4:]
    first = at[0] == 1
    core, row_at = at[1], at[2]
    count, _, wide = up_tiles.shape
    half = outs[0].shape[0] - EXTRA

    def tile(n):
        return pl.ds((part * count + n) * wide, wide)

    def up_copy(n):
        return pltpu.make_async_copy(up.at[:, tile(n)], up_tiles.at[n], sems.at[0, n])

    def down_copy(n):
        return pltpu.make_async_copy(down.at[tile(n)], down_tiles.at[n], sems.at[1, n])

    if part == 0:
        x_copy = pltpu.make_async_copy(x, x_here, sems.at[2, 0])
        x_copy.start()
    for n in range(count):
        up_copy(n).start()

    @pl.when(jnp.logical_not(first))
    def _():
        for n in range(count):
            down_copy(n).start()

    if part == 0:
        x_copy.wait()
        gain_row = gain[...]
        for kk in range(2):

            def prepare(p, carry):
                raw = x_here[(core + kk) % 2, p]
                scaled, stats = norm_stats(raw, gain_row)
                rows = pl.ds(pl.multiple_of((kk * 4 + p) * 32, 32), 32)
                xs_out[rows, :] = jnp.where(first, scaled, raw)
                put_stats(outs[kk], pl.multiple_of(p * 32, 32), wide, stats, row_at)
                return carry

            lax.fori_loop(0, 4, prepare, 0)
        xs_out[pl.ds(2 * half, EXTRA), :] = placed(pieces32(gain_row), row_at).astype(bf16)
        for to in outs[:2]:
            to[pl.ds(half, EXTRA), pl.ds(wide, LANES)] = jnp.zeros((EXTRA, LANES), to.dtype)
        xs = xs_out
    else:
        xs = x

    for n in range(count):
        own, other = outs[2 * n : 2 * n + 2]

        def store(result, extra):
            store_halves(own, other, pl.ds(0, wide), result)
            rows = placed(pieces32(jnp.sum(extra, axis=0, keepdims=True)), row_at)
            own[pl.ds(half, EXTRA), pl.ds(0, wide)] = rows
            other[pl.ds(half, EXTRA), pl.ds(0, wide)] = rows.astype(bf16)

        up_copy(n).wait()

        @pl.when(first)
        def _():
            result = mul(xs[...], up_tiles[n], NN)
            store(result[: 2 * half], result[2 * half :])

        @pl.when(jnp.logical_not(first))
        def _():
            down_copy(n).wait()
            store(
                mul(xs[pl.ds(0, 2 * half), :], down_tiles[n], NT),
                mul(xs[pl.ds(2 * half, EXTRA), :], up_tiles[n], NN),
            )


def quarter_shapes(rows, columns, stats):
    return half_shapes(rows, columns + (LANES if stats else 0)) + half_shapes(rows, columns)


def start_in(at, x, gain, up, down):
    width, hidden = up.shape
    wide, count = hidden // 4, 2
    rows = 128 + EXTRA
    quarters = []
    for part in range(2):
        outs = pl.pallas_call(
            functools.partial(start_kernel, part),
            out_shape=quarter_shapes(rows, wide, part == 0)
            + [jax.ShapeDtypeStruct((256 + EXTRA if part == 0 else 16, width), bf16)],
            in_specs=[SMEM, VMEM if part else HBM, VMEM, HBM, HBM],
            out_specs=[VMEM] * 5,
            scratch_shapes=[
                pltpu.VMEM(x.shape if part == 0 else (16, 128), bf16),
                pltpu.VMEM((count, width, wide), bf16),
                pltpu.VMEM((count, wide, width), bf16),
                pltpu.SemaphoreType.DMA((3, count)),
            ],
            compiler_params=pltpu.CompilerParams(vmem_limit_bytes=16 * 1024 * 1024),
            cost_estimate=pl.CostEstimate(
                flops=256 * width * hidden, bytes_accessed=width * hidden, transcendentals=0
            ),
            name=f"start_in_{part}",
        )(
            at,
            x if part else pltpu.with_memory_space_constraint(x, pltpu.HBM),
            gain,
            pltpu.with_memory_space_constraint(up, pltpu.HBM),
            pltpu.with_memory_space_constraint(down, pltpu.HBM),
        )
        x = outs[4]
        quarters += [outs[0:2], outs[2:4]]
    return quarters


def up_kernel(part, at, x, gain, up, *refs):
    outs, (xs_out, up_tiles, sems) = refs[:4], refs[4:]
    count, _, wide = up_tiles.shape

    def up_copy(n):
        tile = pl.ds((part * count + n) * wide, wide)
        return pltpu.make_async_copy(up.at[:, tile], up_tiles.at[n], sems.at[n])

    for n in range(count):
        up_copy(n).start()
    if part == 0:
        gain_row = gain[...]
        for kk in range(2):

            def prepare(p, carry):
                scaled, stats = norm_stats(x[kk * 4 + p], gain_row)
                xs_out[pl.ds(pl.multiple_of((kk * 4 + p) * 32, 32), 32), :] = scaled
                put_stats(outs[kk], pl.multiple_of(p * 32, 32), wide, stats, at[2])
                return carry

            lax.fori_loop(0, 4, prepare, 0)
    xs = x if part else xs_out
    for n in range(count):
        up_copy(n).wait()
        store_halves(*outs[2 * n : 2 * n + 2], pl.ds(0, wide), mul(xs[...], up_tiles[n], NN))


def up_in(at, x, gain, up):
    width, hidden = up.shape
    wide, count = hidden // 4, 2
    quarters = []
    for part in range(2):
        outs = pl.pallas_call(
            functools.partial(up_kernel, part),
            out_shape=quarter_shapes(128, wide, part == 0)
            + [jax.ShapeDtypeStruct((256 if part == 0 else 16, width), bf16)],
            in_specs=[SMEM, VMEM, VMEM, HBM],
            out_specs=[VMEM] * 5,
            scratch_shapes=[
                pltpu.VMEM((count, width, wide), bf16),
                pltpu.SemaphoreType.DMA((count,)),
            ],
            compiler_params=pltpu.CompilerParams(vmem_limit_bytes=10 * 1024 * 1024),
            cost_estimate=pl.CostEstimate(
                flops=256 * width * hidden, bytes_accessed=width * hidden, transcendentals=0
            ),
            name=f"up_in_{part}",
        )(at, x, gain, pltpu.with_memory_space_constraint(up, pltpu.HBM))
        x = outs[4]
        quarters += [outs[0:2], outs[2:4]]
    return quarters


def down_back_kernel(part, x, down, *outs):
    wide = outs[0].shape[1]
    for n in range(2):
        result = mul(x[...], down[pl.ds((2 * part + n) * wide, wide), :], NT)
        store_halves(*outs[2 * n : 2 * n + 2], pl.ds(0, wide), result)


def local_call(kernel, shapes, operands, name, flops, nbytes, smem=False, scratch=()):
    specs = [SMEM if smem and i == 0 else VMEM for i in range(len(operands))]
    return pl.pallas_call(
        kernel,
        out_shape=shapes,
        in_specs=specs,
        out_specs=[VMEM] * len(shapes),
        scratch_shapes=list(scratch),
        compiler_params=pltpu.CompilerParams(vmem_limit_bytes=6 * 1024 * 1024),
        cost_estimate=pl.CostEstimate(flops=flops, bytes_accessed=nbytes, transcendentals=0),
        name=name,
    )(*operands)


def half_shapes(rows, columns):
    return [
        jax.ShapeDtypeStruct((rows, columns), f32),
        jax.ShapeDtypeStruct((rows, columns), bf16),
    ]


def down_back_in(x, down):
    hidden, width = down.shape
    quarters = []
    for part in range(2):
        outs = local_call(
            functools.partial(down_back_kernel, part),
            quarter_shapes(128, hidden // 4, False),
            (x.reshape(256, width), down),
            f"down_back_{part}",
            256 * width * hidden,
            width * hidden,
        )
        quarters += [outs[0:2], outs[2:4]]
    return quarters


def row_out_kernel(mode, at, *refs):
    inputs, rest, (out, xs) = refs[:8], refs[8:-2], refs[-2:]
    first = at[0] == 1
    half, columns = 128, xs.shape[1] // 4
    width = out.shape[-1]
    slot = 0
    for i in range(2):
        for j in range(4):
            ref = inputs[4 * i + j]
            xs[pl.ds(i * half, half), pl.ds(j * columns, columns)] = ref[:, pl.ds(0, columns)]

    def terms():
        gain, x = rest[:2]
        for i in range(2):
            early, late = (inputs[4 * i + j][:, pl.ds(columns, LANES)].astype(f32) for j in (1, 3))
            ext = early + late
            first0, second0, first1, second1, mean, inv_std = (
                ext[:, 3 * k : 3 * k + 1] + ext[:, 3 * k + 1 : 3 * k + 2] + ext[:, 3 * k + 2 : 3 * k + 3]
                for k in range(6)
            )
            for p in range(4):
                pick = slice(p * 32, p * 32 + 32)
                yield (
                    i * 4 + p,
                    gain,
                    x.at[(at[1] + i) % 2, p] if mode == 2 else x.at[i * 4 + p],
                    (first0 + first1)[pick],
                    (second0 + second1)[pick],
                    mean[pick],
                    inv_std[pick],
                )

    def steps(weight, dims, back):
        saved = list(terms()) if back else []

        def step(n, carry):
            at_n = pl.ds(pl.multiple_of(n * 512, 512), 512)
            tile = weight[:, at_n] if dims is NN else weight[at_n, :]
            result = mul(xs[...], tile, dims)
            if not back:
                for k in range(8):
                    out[slot + k, :, at_n] = result[k * 32 : k * 32 + 32].astype(bf16)
            for k, gain, x, first_sum, second_sum, mean, inv_std in saved:
                grad = result[k * 32 : k * 32 + 32] * gain[:, at_n]
                normed = (x[:, at_n].astype(f32) - mean) * inv_std
                out[slot + k, :, at_n] = (inv_std * (grad - first_sum - normed * second_sum)).astype(bf16)
            return carry

        lax.fori_loop(0, width // 512, step, 0)

    if mode == 0:
        steps(rest[0], NN, False)
    elif mode == 1:
        steps(rest[2], NT, True)
    else:
        pl.when(first)(lambda: steps(rest[2], NT, True))
        pl.when(jnp.logical_not(first))(lambda: steps(rest[3], NN, False))


def row_out(mode, at, mine, others, rest):
    hidden, width = max(rest[-1].shape), min(rest[-1].shape)
    (out,) = local_call(
        functools.partial(row_out_kernel, mode),
        [jax.ShapeDtypeStruct((8, 32, width), bf16)],
        (at, *mine, *others, *rest),
        f"row_out_{mode}",
        2 * 256 * width * hidden,
        2 * width * hidden,
        smem=True,
        scratch=[pltpu.VMEM((256, hidden), bf16)],
    )
    return out


def finish_kernel(parts, base, out):
    total = base[...].astype(f32)
    for k in range(8):
        total = total + parts[k].astype(f32)
    total = total.astype(bf16)
    if len(out.shape) == 2:
        out[...] = total
    else:
        for k in range(8):
            out[k] = total


def finish(parts, base, copies):
    block, width = base.shape
    (out,) = local_call(
        finish_kernel,
        [jax.ShapeDtypeStruct((8, block, width) if copies else base.shape, bf16)],
        (parts, base),
        "finish",
        8 * block * width,
        20 * block * width,
    )
    return out


def permuted(array, axis, mapping):
    return lax.ppermute(array, axis, [(i, mapping(i)) for i in range(lax.axis_size(axis))])


def body(section_feeds, norm_gain, up_weight, down_weight):
    up = up_weight[0]
    down = down_weight[0]
    gain = norm_gain
    width, hidden = up.shape
    micro, rows = section_feeds.shape[1], section_feeds.shape[2]
    rsize, tsize = lax.axis_size("row"), lax.axis_size("tp")
    total_width = width * rsize
    tokens = micro * rows
    block = tokens // tsize
    is_first = lax.axis_index("section") == 0
    row_at = lax.axis_index("row")
    tp_at = lax.axis_index("tp")
    core = row_at % 2
    lane = lax.broadcasted_iota(jnp.int32, (1, LANES), 1)
    at = jnp.stack([is_first.astype(jnp.int32), core, row_at])

    def to_global(array):
        blocks = array.reshape(micro, rows, width)
        return jnp.where(core == 0, blocks, blocks[::-1])

    def pair(i):
        return i ^ 1

    def near(i):
        return i ^ 2

    def far(i):
        return i ^ 6

    def row_sum(quarters):
        sums = [own + permuted(other, "row", pair).astype(f32) for own, other in quarters]
        for ways in ((near, far, near, far), (far, near, far, near)):
            arrived = [permuted(h.astype(bf16), "row", way) for h, way in zip(sums, ways)]
            sums = [h + r.astype(f32) for h, r in zip(sums, arrived)]
        return sums

    def swapped(chunks):
        return chunks, [permuted(chunk, "row", pair) for chunk in chunks]

    def along_tp(part):
        return lax.all_to_all(part, "tp", 0, 0)

    def norm_of(ext):
        means = ext[:, :rsize] + ext[:, rsize : 2 * rsize] + ext[:, 2 * rsize : 3 * rsize]
        squares = (
            ext[:, 3 * rsize : 4 * rsize]
            + ext[:, 4 * rsize : 5 * rsize]
            + ext[:, 5 * rsize : 6 * rsize]
        )
        mean = jnp.sum(means, axis=1, keepdims=True) / rsize
        shift = means - mean
        variance = jnp.sum(squares + width * shift * shift, axis=1, keepdims=True) / total_width
        return mean, lax.rsqrt(variance + epsilon), shift

    def normed_pre(summed, part, stats):
        _, inv_std, shift = stats
        fixed = summed
        for i in range(rsize):
            fixed = fixed + shift[:, i : i + 1] * gain_rows[part][i]
        return inv_std * fixed

    def back_sums(pre_grad, pre, part):
        grads = pre_grad.astype(f32)
        return (
            jnp.sum(grads * gain_total[part], axis=1, keepdims=True) / total_width,
            jnp.sum(grads * pre, axis=1, keepdims=True) / total_width,
        )

    def back_chunks(chunks, sums, stats):
        chunks = list(chunks)
        for part in (1, 3):
            values = [a + b for a, b in zip(sums[part - 1], sums[part])]
            spot = 0 if part == 1 else 6
            out = jnp.zeros((rows, LANES), f32)
            for value in values + ([] if part == 1 else list(stats[:2])):
                for piece in pieces32(value):
                    out = out + jnp.where(lane == spot, piece, 0.0)
                    spot += 1
            chunks[part] = jnp.concatenate([chunks[part], out.astype(bf16)], axis=1)
        return chunks

    blocks = rows // block
    feeds = section_feeds[0].reshape(micro, blocks, block, width)
    own_feed = lax.dynamic_slice(
        feeds, ((core + tp_at // blocks) % 2, tp_at % blocks, 0, 0), (1, 1, block, width)
    )[0, 0]
    sums = row_sum(start_in(at, feeds, gain, up, down))
    columns = hidden // 4
    gain_rows = [
        [
            jnp.sum(part[rows + 3 * i : rows + 3 * i + 3, :columns], axis=0, keepdims=True)
            for i in range(rsize)
        ]
        for part in sums
    ]
    gain_total = [sum(part) for part in gain_rows]
    stats0 = norm_of(sums[0][:rows, columns:])
    hidden_grad1 = [part[:rows, :columns] for part in sums]
    pre0 = [normed_pre(hidden_grad1[part], part, stats0) for part in range(4)]
    chunks = [gelu_value(pre).astype(bf16) for pre in pre0]
    parts = along_tp(row_out(0, at, *swapped(chunks), (down,)))
    middle = lax.ppermute(finish(parts, own_feed, False), "section", [(0, 1)])
    middles = along_tp(jnp.broadcast_to(middle[None], (tsize,) + middle.shape))

    sums = row_sum(up_in(at, middles, gain, up))
    stats1 = norm_of(sums[0][:, columns:])
    hidden1, chunks, terms = [], [], []
    for part in range(4):
        pre = normed_pre(sums[part][:, :columns], part, stats1)
        hidden1.append(gelu_value(pre).astype(bf16))
        chunks.append((hidden_grad1[part] * gelu_slope(pre)).astype(bf16))
        terms.append(back_sums(chunks[part], pre, part))
    chunks = back_chunks(chunks, terms, stats1)
    parts = along_tp(row_out(1, at, *swapped(chunks), (gain, middles, up)))
    back = lax.ppermute(finish(parts, own_feed, False), "section", [(1, 0)])
    backs = along_tp(jnp.broadcast_to(back[None], (tsize,) + back.shape))

    sums = row_sum(down_back_in(backs, down))
    chunks, terms = [], []
    for part in range(4):
        pre_grad = (sums[part] * gelu_slope(pre0[part])).astype(bf16)
        chunks.append(jnp.where(is_first, pre_grad, hidden1[part]))
        terms.append(back_sums(pre_grad, pre0[part], part))
    chunks = back_chunks(chunks, terms, stats0)
    parts = along_tp(row_out(2, at, *swapped(chunks), (gain, feeds, up, down)))
    base = jnp.where(is_first, back, middle)
    return to_global(along_tp(finish(parts, base, True)))[None]


def solution(mesh):
    placed = (
        P("section", None, None, "row"),
        P("section", "row"),
        P("section", "row", "tp"),
        P("section", "tp", "row"),
    )
    return jax.shard_map(
        body, mesh=mesh, in_specs=placed, out_specs=P("section", None, None, "row"), check_vma=False
    )
```

```python
import functools

import jax
import jax.numpy as jnp
from jax import lax
from jax.experimental import pallas as pl
from jax.experimental.pallas import tpu as pltpu
from jax.sharding import PartitionSpec as P

epsilon = 1e-05
gelu_coeff = 0.7978845608028654
LANES = 128
EXTRA = 32
f32 = jnp.float32
bf16 = jnp.bfloat16
NN = (((1,), (0,)), ((), ()))
NT = (((1,), (1,)), ((), ()))
HBM = pl.BlockSpec(memory_space=pltpu.HBM)
VMEM = pl.BlockSpec(memory_space=pltpu.VMEM)
SMEM = pl.BlockSpec(memory_space=pltpu.SMEM)


def gelu_tangent(inputs):
    return jnp.tanh(gelu_coeff * (inputs + 0.044715 * inputs * inputs * inputs))


def gelu_value(inputs):
    return 0.5 * inputs * (1.0 + gelu_tangent(inputs))


def pieces(value):
    high = value.astype(bf16)
    rest = value - high.astype(f32)
    middle = rest.astype(bf16)
    low = (rest - middle.astype(f32)).astype(bf16)
    return high, middle, low


def pieces32(value):
    return tuple(part.astype(f32) for part in pieces(value))


def mul(a, b, dims):
    return lax.dot_general(a, b, dims, preferred_element_type=f32)


def norm_stats(raw, gain_row):
    values = raw.astype(f32)
    mean = jnp.sum(values, axis=1, keepdims=True) / values.shape[1]
    centred = values - mean
    squares = jnp.sum(centred * centred, axis=1, keepdims=True)
    return (centred * gain_row).astype(bf16), pieces32(mean) + pieces32(squares)


def put_stats(to, start, lanes, stats, row_at):
    lane = lax.broadcasted_iota(jnp.int32, (1, LANES), 1)
    ext = jnp.zeros((stats[0].shape[0], LANES), f32)
    for i, part in enumerate(stats):
        ext = ext + jnp.where(lane == i * 8 + row_at, part, 0.0)
    to[pl.ds(start, ext.shape[0]), pl.ds(lanes, LANES)] = ext.astype(to.dtype)


def placed(parts, row_at):
    spot = lax.broadcasted_iota(jnp.int32, (EXTRA, 1), 0)
    return sum(jnp.where(spot == 3 * row_at + j, part, 0.0) for j, part in enumerate(parts))


def store_halves(own, other, columns, result):
    half = result.shape[0] // 2
    own[pl.ds(0, half), columns] = result[:half]
    other[pl.ds(0, half), columns] = result[half:].astype(bf16)


def start_kernel(part, at, x, gain, up, down, *refs):
    outs, (xs_out, x_here, up_tiles, down_tiles, sems) = refs[:2], refs[2:]
    own, other = outs
    first = at[0] == 1
    core, row_at = at[1], at[2]
    count, _, wide = up_tiles.shape
    half = outs[0].shape[0] - EXTRA

    def tile(n):
        return pl.ds((part * count + n) * wide, wide)

    def up_copy(n):
        return pltpu.make_async_copy(up.at[:, tile(n)], up_tiles.at[n], sems.at[0, n])

    def down_copy(n):
        return pltpu.make_async_copy(down.at[tile(n)], down_tiles.at[n], sems.at[1, n])

    if part == 0:
        x_copy = pltpu.make_async_copy(x, x_here, sems.at[2, 0])
        x_copy.start()
    for n in range(count):
        up_copy(n).start()

    @pl.when(jnp.logical_not(first))
    def _():
        for n in range(count):
            down_copy(n).start()

    if part == 0:
        x_copy.wait()
        gain_row = gain[...]
        for kk in range(2):

            def prepare(p, carry):
                raw = x_here[(core + kk) % 2, p]
                scaled, stats = norm_stats(raw, gain_row)
                rows = pl.ds(pl.multiple_of((kk * 4 + p) * 32, 32), 32)
                xs_out[rows, :] = jnp.where(first, scaled, raw)
                put_stats(outs[kk], pl.multiple_of(p * 32, 32), count * wide, stats, row_at)
                return carry

            lax.fori_loop(0, 4, prepare, 0)
        xs_out[pl.ds(2 * half, EXTRA), :] = placed(pieces32(gain_row), row_at).astype(bf16)
        for to in outs[:2]:
            to[pl.ds(half, EXTRA), pl.ds(count * wide, LANES)] = jnp.zeros((EXTRA, LANES), to.dtype)
        xs = xs_out
    else:
        xs = x

    for n in range(count):

        def store(columns, result, extra):
            store_halves(own, other, columns, result)
            rows = placed(pieces32(jnp.sum(extra, axis=0, keepdims=True)), row_at)
            own[pl.ds(half, EXTRA), columns] = rows
            other[pl.ds(half, EXTRA), columns] = rows.astype(bf16)

        up_copy(n).wait()

        @pl.when(first)
        def _():
            result = mul(xs[...], up_tiles[n], NN)
            store(pl.ds(n * wide, wide), result[: 2 * half], result[2 * half :])

        @pl.when(jnp.logical_not(first))
        def _():
            down_copy(n).wait()

            def piece(i, carry):
                columns = pl.ds(pl.multiple_of(i * 256, 256), 256)
                store(
                    pl.ds(pl.multiple_of(n * wide + i * 256, 256), 256),
                    mul(xs[pl.ds(0, 2 * half), :], down_tiles[n, columns], NT),
                    mul(xs[pl.ds(2 * half, EXTRA), :], up_tiles[n, :, columns], NN),
                )
                return carry

            lax.fori_loop(0, wide // 256, piece, 0)


def start_in(at, x, gain, up, down):
    width, hidden = up.shape
    wide, count = hidden // 4, 2
    rows = 128 + EXTRA
    halves = []
    for part in range(2):
        outs = pl.pallas_call(
            functools.partial(start_kernel, part),
            out_shape=half_shapes(rows, count * wide + (0 if part else LANES))
            + [jax.ShapeDtypeStruct((256 + EXTRA if part == 0 else 16, width), bf16)],
            in_specs=[SMEM, VMEM if part else HBM, VMEM, HBM, HBM],
            out_specs=[VMEM] * 3,
            scratch_shapes=[
                pltpu.VMEM(x.shape if part == 0 else (16, 128), bf16),
                pltpu.VMEM((count, width, wide), bf16),
                pltpu.VMEM((count, wide, width), bf16),
                pltpu.SemaphoreType.DMA((3, count)),
            ],
            compiler_params=pltpu.CompilerParams(vmem_limit_bytes=16 * 1024 * 1024),
            cost_estimate=pl.CostEstimate(
                flops=256 * width * hidden, bytes_accessed=width * hidden, transcendentals=0
            ),
            name=f"start_in_{part}",
        )(
            at,
            x if part else pltpu.with_memory_space_constraint(x, pltpu.HBM),
            gain,
            pltpu.with_memory_space_constraint(up, pltpu.HBM),
            pltpu.with_memory_space_constraint(down, pltpu.HBM),
        )
        x = outs[2]
        halves.append(outs[:2])
    return halves


def up_kernel(part, at, x, gain, up, *refs):
    outs, (xs_out, up_tiles, sems) = refs[:2], refs[2:]
    count, _, wide = up_tiles.shape

    def up_copy(n):
        tile = pl.ds((part * count + n) * wide, wide)
        return pltpu.make_async_copy(up.at[:, tile], up_tiles.at[n], sems.at[n])

    for n in range(count):
        up_copy(n).start()
    if part == 0:
        gain_row = gain[...]
        for kk in range(2):

            def prepare(p, carry):
                scaled, stats = norm_stats(x[kk * 4 + p], gain_row)
                xs_out[pl.ds(pl.multiple_of((kk * 4 + p) * 32, 32), 32), :] = scaled
                put_stats(outs[kk], pl.multiple_of(p * 32, 32), count * wide, stats, at[2])
                return carry

            lax.fori_loop(0, 4, prepare, 0)
    xs = x if part else xs_out
    for n in range(count):
        up_copy(n).wait()
        store_halves(*outs, pl.ds(n * wide, wide), mul(xs[...], up_tiles[n], NN))


def up_in(at, x, gain, up):
    width, hidden = up.shape
    wide, count = hidden // 4, 2
    halves = []
    for part in range(2):
        outs = pl.pallas_call(
            functools.partial(up_kernel, part),
            out_shape=half_shapes(128, count * wide + (0 if part else LANES))
            + [jax.ShapeDtypeStruct((256 if part == 0 else 16, width), bf16)],
            in_specs=[SMEM, VMEM, VMEM, HBM],
            out_specs=[VMEM] * 3,
            scratch_shapes=[
                pltpu.VMEM((count, width, wide), bf16),
                pltpu.SemaphoreType.DMA((count,)),
            ],
            compiler_params=pltpu.CompilerParams(vmem_limit_bytes=10 * 1024 * 1024),
            cost_estimate=pl.CostEstimate(
                flops=256 * width * hidden, bytes_accessed=width * hidden, transcendentals=0
            ),
            name=f"up_in_{part}",
        )(at, x, gain, pltpu.with_memory_space_constraint(up, pltpu.HBM))
        x = outs[2]
        halves.append(outs[:2])
    return halves


def down_back_kernel(part, x, down, own, other):
    wide = own.shape[1] // 2
    for n in range(2):
        result = mul(x[...], down[pl.ds((2 * part + n) * wide, wide), :], NT)
        store_halves(own, other, pl.ds(n * wide, wide), result)


def local_call(kernel, shapes, operands, name, flops, nbytes, smem=False, scratch=()):
    specs = [SMEM if smem and i == 0 else VMEM for i in range(len(operands))]
    return pl.pallas_call(
        kernel,
        out_shape=shapes,
        in_specs=specs,
        out_specs=[VMEM] * len(shapes),
        scratch_shapes=list(scratch),
        compiler_params=pltpu.CompilerParams(vmem_limit_bytes=6 * 1024 * 1024),
        cost_estimate=pl.CostEstimate(flops=flops, bytes_accessed=nbytes, transcendentals=0),
        name=name,
    )(*operands)


def half_shapes(rows, columns):
    return [
        jax.ShapeDtypeStruct((rows, columns), f32),
        jax.ShapeDtypeStruct((rows, columns), bf16),
    ]


def down_back_in(x, down):
    hidden, width = down.shape
    halves = []
    for part in range(2):
        outs = local_call(
            functools.partial(down_back_kernel, part),
            half_shapes(128, hidden // 2),
            (x.reshape(256, width), down),
            f"down_back_{part}",
            256 * width * hidden,
            width * hidden,
        )
        halves.append(outs)
    return halves


def row_out_kernel(mode, at, *refs):
    inputs, rest, (out, xs) = refs[:4], refs[4:-2], refs[-2:]
    first = at[0] == 1
    half, columns = 128, xs.shape[1] // 2
    width = out.shape[-1]
    slot = 0
    for i in range(2):
        for j in range(2):
            ref = inputs[2 * i + j]
            xs[pl.ds(i * half, half), pl.ds(j * columns, columns)] = ref[:, pl.ds(0, columns)]

    def terms():
        gain, x = rest[:2]
        for i in range(2):
            early, late = (r[:, pl.ds(columns, LANES)].astype(f32) for r in inputs[2 * i : 2 * i + 2])
            ext = early + late
            first0, second0, first1, second1, mean, inv_std = (
                ext[:, 3 * k : 3 * k + 1] + ext[:, 3 * k + 1 : 3 * k + 2] + ext[:, 3 * k + 2 : 3 * k + 3]
                for k in range(6)
            )
            for p in range(4):
                pick = slice(p * 32, p * 32 + 32)
                yield (
                    i * 4 + p,
                    gain,
                    x.at[(at[1] + i) % 2, p] if mode == 2 else x.at[i * 4 + p],
                    (first0 + first1)[pick],
                    (second0 + second1)[pick],
                    mean[pick],
                    inv_std[pick],
                )

    def steps(weight, dims, back):
        saved = list(terms()) if back else []

        def step(n, carry):
            at_n = pl.ds(pl.multiple_of(n * 512, 512), 512)
            tile = weight[:, at_n] if dims is NN else weight[at_n, :]
            result = mul(xs[...], tile, dims)
            if not back:
                for k in range(8):
                    out[slot + k, :, at_n] = result[k * 32 : k * 32 + 32].astype(bf16)
            for k, gain, x, first_sum, second_sum, mean, inv_std in saved:
                grad = result[k * 32 : k * 32 + 32] * gain[:, at_n]
                normed = (x[:, at_n].astype(f32) - mean) * inv_std
                out[slot + k, :, at_n] = (inv_std * (grad - first_sum - normed * second_sum)).astype(bf16)
            return carry

        lax.fori_loop(0, width // 512, step, 0)

    if mode == 0:
        steps(rest[0], NN, False)
    elif mode == 1:
        steps(rest[2], NT, True)
    else:
        pl.when(first)(lambda: steps(rest[2], NT, True))
        pl.when(jnp.logical_not(first))(lambda: steps(rest[3], NN, False))


def row_out(mode, at, mine, others, rest):
    hidden, width = max(rest[-1].shape), min(rest[-1].shape)
    (out,) = local_call(
        functools.partial(row_out_kernel, mode),
        [jax.ShapeDtypeStruct((8, 32, width), bf16)],
        (at, *mine, *others, *rest),
        f"row_out_{mode}",
        2 * 256 * width * hidden,
        2 * width * hidden,
        smem=True,
        scratch=[pltpu.VMEM((256, hidden), bf16)],
    )
    return out


MEAN, INV, SHIFT = 0, 1, 8


def act_kernel(mode, part, at, *refs):
    refs = list(refs)
    first = at[0] == 1
    sums = [(refs.pop(0), refs.pop(0)) for _ in range(2)]
    stats = refs.pop(0) if mode == 2 or part else None
    gains = refs.pop(0) if mode else None
    saved = refs.pop(0) if mode else None
    hidden = refs.pop(0) if mode == 2 else None
    chunk = refs.pop(0)
    saved_out = refs.pop(0) if mode == 0 else None
    hidden_out = refs.pop(0) if mode == 1 else None
    gains_out = refs.pop(0) if mode == 0 else None
    stats_out = refs.pop(0) if mode != 2 and part == 0 else None
    wide = 1024
    total_width = 8192
    lane = lax.broadcasted_iota(jnp.int32, (1, LANES), 1)
    if mode == 0:
        gains = gains_out
        for q, (held, arrived) in enumerate(sums):
            columns = pl.ds(q * wide, wide)
            extra = held[pl.ds(128, EXTRA), pl.ds(0, wide)] + arrived[pl.ds(128, EXTRA), pl.ds(0, wide)].astype(f32)
            for r in range(8):
                gains[pl.ds(r, 1), columns] = jnp.sum(extra[3 * r : 3 * r + 3], axis=0, keepdims=True)
    if stats_out is not None:
        stats = stats_out
        held, arrived = sums[1]
        ext = held[pl.ds(0, 128), pl.ds(wide, LANES)] + arrived[pl.ds(0, 128), pl.ds(wide, LANES)].astype(f32)
        means = [sum(ext[:, 8 * k + r : 8 * k + r + 1] for k in range(3)) for r in range(8)]
        mean = sum(means) / 8
        shifts = [value - mean for value in means]
        squares = jnp.sum(jnp.where((lane >= 24) & (lane < 48), ext, 0.0), axis=1, keepdims=True)
        variance = (squares + wide * sum(value * value for value in shifts)) / total_width
        inv_std = lax.rsqrt(variance + epsilon)
        if mode == 0:
            inv_std = jnp.where(first, inv_std, 1.0)
            shifts = [jnp.where(first, value, 0.0) for value in shifts]
        out = jnp.where(lane == MEAN, mean, 0.0) + jnp.where(lane == INV, inv_std, 0.0)
        for r, value in enumerate(shifts):
            out = out + jnp.where(lane == SHIFT + r, value, 0.0)
        stats[...] = out

    size, span = 16, 512

    def block(i, carry):
        rows = pl.ds(pl.multiple_of(i * size, size), size)
        here = stats[rows, :]
        mean, inv_std = here[:, MEAN : MEAN + 1], here[:, INV : INV + 1]
        shifts = [here[:, SHIFT + r : SHIFT + r + 1] for r in range(8)]
        firsts = jnp.zeros((size, span), f32)
        seconds = jnp.zeros((size, span), f32)
        for n in range(2 * wide // span):
            columns = pl.ds(n * span, span)
            held, arrived = sums[n * span // wide]
            inner = pl.ds(n * span % wide, span)
            value = held[rows, inner] + arrived[rows, inner].astype(f32)
            if mode != 2:
                for r in range(8):
                    value = value + shifts[r] * gains[pl.ds(r, 1), columns]
                value = inv_std * value
            pre = saved[rows, columns] if mode == 2 else value
            if mode == 0:
                saved_out[rows, columns] = pre
                chunk[rows, columns] = gelu_value(pre).astype(bf16)
                continue
            tangent = gelu_tangent(pre)
            slope = 0.5 * (1.0 + tangent) + 0.5 * pre * (1.0 - tangent * tangent) * gelu_coeff * (
                1.0 + 3.0 * 0.044715 * pre * pre
            )
            grad = (value if mode == 2 else saved[rows, columns]) * slope
            grad_sent = grad.astype(bf16)
            if mode == 1:
                hidden_out[rows, columns] = (0.5 * pre * (1.0 + tangent)).astype(bf16)
                chunk[rows, columns] = grad_sent
            else:
                chunk[rows, columns] = jnp.where(first, grad_sent, hidden[rows, columns])
            grad = grad_sent.astype(f32)
            gain_sum = jnp.sum(gains[:, columns], axis=0, keepdims=True)
            firsts = firsts + grad * gain_sum
            seconds = seconds + grad * pre
        if mode:
            values = [
                jnp.sum(v, axis=1, keepdims=True) / total_width for v in (firsts, seconds)
            ] + ([mean, inv_std] if part else [])
            ext = jnp.zeros((size, LANES), f32)
            spot = 6 * part
            for value in values:
                for piece in pieces32(value):
                    ext = ext + jnp.where(lane == spot, piece, 0.0)
                    spot += 1
            chunk[rows, pl.ds(2 * wide, LANES)] = ext.astype(bf16)
        return carry

    lax.fori_loop(0, 128 // size, block, 0)


def act(mode, part, at, sums, stats, gains, saved, hidden):
    wide = 2048
    operands = [at] + [ref for pair in sums for ref in pair]
    if mode == 2 or part:
        operands.append(stats)
    if mode:
        operands += [gains, saved]
    if mode == 2:
        operands.append(hidden)
    shapes = [jax.ShapeDtypeStruct((128, wide + (LANES if mode else 0)), bf16)]
    if mode == 0:
        shapes.append(jax.ShapeDtypeStruct((128, wide), f32))
    if mode == 1:
        shapes.append(jax.ShapeDtypeStruct((128, wide), bf16))
    if mode == 0:
        shapes.append(jax.ShapeDtypeStruct((8, wide), f32))
    if mode != 2 and part == 0:
        shapes.append(jax.ShapeDtypeStruct((128, LANES), f32))
    return local_call(
        functools.partial(act_kernel, mode, part),
        shapes,
        operands,
        f"act_{mode}_{part}",
        40 * 128 * wide,
        16 * 128 * wide,
        smem=True,
    )


def finish_kernel(parts, base, out):
    total = base[...].astype(f32)
    for k in range(8):
        total = total + parts[k].astype(f32)
    total = total.astype(bf16)
    if len(out.shape) == 2:
        out[...] = total
    else:
        for k in range(8):
            out[k] = total


def finish(parts, base, copies):
    block, width = base.shape
    (out,) = local_call(
        finish_kernel,
        [jax.ShapeDtypeStruct((8, block, width) if copies else base.shape, bf16)],
        (parts, base),
        "finish",
        8 * block * width,
        20 * block * width,
    )
    return out


def permuted(array, axis, mapping):
    return lax.ppermute(array, axis, [(i, mapping(i)) for i in range(lax.axis_size(axis))])


def body(section_feeds, norm_gain, up_weight, down_weight):
    up = up_weight[0]
    down = down_weight[0]
    gain = norm_gain
    width, hidden = up.shape
    micro, rows = section_feeds.shape[1], section_feeds.shape[2]
    rsize, tsize = lax.axis_size("row"), lax.axis_size("tp")
    tokens = micro * rows
    block = tokens // tsize
    is_first = lax.axis_index("section") == 0
    row_at = lax.axis_index("row")
    tp_at = lax.axis_index("tp")
    core = row_at % 2
    at = jnp.stack([is_first.astype(jnp.int32), core, row_at])

    def to_global(array):
        blocks = array.reshape(micro, rows, width)
        return jnp.where(core == 0, blocks, blocks[::-1])

    def pair(i):
        return i ^ 1

    def near(i):
        return i ^ 2

    def far(i):
        return i ^ 6

    def row_sum(halves):
        sums = []
        for own, other in halves:
            arrived = permuted(other, "row", pair)
            for columns in (slice(0, hidden // 4), slice(hidden // 4, None)):
                sums.append(own[:, columns] + arrived[:, columns].astype(f32))
        ways = (near, far, near, far)
        arrived = [permuted(h.astype(bf16), "row", way) for h, way in zip(sums, ways)]
        sums = [h + r.astype(f32) for h, r in zip(sums, arrived)]
        ways = (far, near, far, near)
        arrived = [permuted(h.astype(bf16), "row", way) for h, way in zip(sums, ways)]
        quarters = list(zip(sums, arrived))
        return quarters[:2], quarters[2:]

    def swapped(chunks):
        return chunks, [permuted(chunk, "row", pair) for chunk in chunks]

    def along_tp(part):
        return lax.all_to_all(part, "tp", 0, 0)

    blocks = rows // block
    feeds = section_feeds[0].reshape(micro, blocks, block, width)
    own_feed = lax.dynamic_slice(
        feeds, ((core + tp_at // blocks) % 2, tp_at % blocks, 0, 0), (1, 1, block, width)
    )[0, 0]
    early, late = row_sum(start_in(at, feeds, gain, up, down))
    chunk, saved, gains, stats0 = act(0, 0, at, early, None, None, None, None)
    chunks, saved0, gain_rows = [chunk], [saved], [gains]
    chunk, saved, gains = act(0, 1, at, late, stats0, None, None, None)
    chunks, saved0, gain_rows = chunks + [chunk], saved0 + [saved], gain_rows + [gains]
    parts = along_tp(row_out(0, at, *swapped(chunks), (down,)))
    middle = lax.ppermute(finish(parts, own_feed, False), "section", [(0, 1)])
    middles = along_tp(jnp.broadcast_to(middle[None], (tsize,) + middle.shape))

    early, late = row_sum(up_in(at, middles, gain, up))
    chunk0, hidden0, stats1 = act(1, 0, at, early, None, gain_rows[0], saved0[0], None)
    chunk1, hidden1 = act(1, 1, at, late, stats1, gain_rows[1], saved0[1], None)
    chunks = [chunk0, chunk1]
    parts = along_tp(row_out(1, at, *swapped(chunks), (gain, middles, up)))
    back = lax.ppermute(finish(parts, own_feed, False), "section", [(1, 0)])
    backs = along_tp(jnp.broadcast_to(back[None], (tsize,) + back.shape))

    early, late = row_sum(down_back_in(backs, down))
    chunks = []
    for part, sums in enumerate((early, late)):
        kept = (hidden0, hidden1)[part]
        (chunk,) = act(2, part, at, sums, stats0, gain_rows[part], saved0[part], kept)
        chunks.append(chunk)
    parts = along_tp(row_out(2, at, *swapped(chunks), (gain, feeds, up, down)))
    base = jnp.where(is_first, back, middle)
    return to_global(along_tp(finish(parts, base, True)))[None]


def solution(mesh):
    placed = (
        P("section", None, None, "row"),
        P("section", "row"),
        P("section", "row", "tp"),
        P("section", "tp", "row"),
    )
    return jax.shard_map(
        body, mesh=mesh, in_specs=placed, out_specs=P("section", None, None, "row"), check_vma=False
    )
```

```python
import functools

import jax
import jax.numpy as jnp
from jax import lax
from jax.experimental import pallas as pl
from jax.experimental.pallas import tpu as pltpu
from jax.sharding import PartitionSpec as P

epsilon = 1e-05
gelu_coeff = 0.7978845608028654
LANES = 128
EXTRA = 32
f32 = jnp.float32
bf16 = jnp.bfloat16
NN = (((1,), (0,)), ((), ()))
NT = (((1,), (1,)), ((), ()))
HBM = pl.BlockSpec(memory_space=pltpu.HBM)
VMEM = pl.BlockSpec(memory_space=pltpu.VMEM)
SMEM = pl.BlockSpec(memory_space=pltpu.SMEM)


def gelu_tangent(inputs):
    return jnp.tanh(gelu_coeff * (inputs + 0.044715 * inputs * inputs * inputs))


def gelu_value(inputs):
    return 0.5 * inputs * (1.0 + gelu_tangent(inputs))


def pieces(value):
    high = value.astype(bf16)
    rest = value - high.astype(f32)
    middle = rest.astype(bf16)
    low = (rest - middle.astype(f32)).astype(bf16)
    return high, middle, low


def pieces32(value):
    return tuple(part.astype(f32) for part in pieces(value))


def mul(a, b, dims):
    return lax.dot_general(a, b, dims, preferred_element_type=f32)


def norm_stats(raw, gain_row):
    values = raw.astype(f32)
    mean = jnp.sum(values, axis=1, keepdims=True) / values.shape[1]
    centred = values - mean
    squares = jnp.sum(centred * centred, axis=1, keepdims=True)
    return (centred * gain_row).astype(bf16), pieces32(mean) + pieces32(squares)


def put_stats(to, start, lanes, stats, row_at):
    lane = lax.broadcasted_iota(jnp.int32, (1, LANES), 1)
    ext = jnp.zeros((stats[0].shape[0], LANES), f32)
    for i, part in enumerate(stats):
        ext = ext + jnp.where(lane == i * 8 + row_at, part, 0.0)
    to[pl.ds(start, ext.shape[0]), pl.ds(lanes, LANES)] = ext.astype(to.dtype)


def placed(parts, row_at):
    spot = lax.broadcasted_iota(jnp.int32, (EXTRA, 1), 0)
    return sum(jnp.where(spot == 3 * row_at + j, part, 0.0) for j, part in enumerate(parts))


def store_halves(own, other, columns, result):
    half = result.shape[0] // 2
    own[pl.ds(0, half), columns] = result[:half]
    other[pl.ds(0, half), columns] = result[half:].astype(bf16)


def start_kernel(at, x, gain, up, down, *refs):
    outs, (xs, x_here, gain_here, up_tiles, down_tiles, sems) = refs[:4], refs[4:]
    first = at[0] == 1
    core, row_at = at[1], at[2]
    count, _, wide = up_tiles.shape
    half = outs[0].shape[0] - EXTRA
    columns = outs[2].shape[1]

    def up_copy(n):
        return pltpu.make_async_copy(up.at[:, pl.ds(n * wide, wide)], up_tiles.at[n], sems.at[0, n])

    def down_copy(n):
        return pltpu.make_async_copy(down.at[pl.ds(n * wide, wide)], down_tiles.at[n], sems.at[1, n])

    x_copy = pltpu.make_async_copy(x, x_here, sems.at[2, 0])
    gain_copy = pltpu.make_async_copy(gain, gain_here, sems.at[2, 1])
    x_copy.start()
    gain_copy.start()

    @pl.when(jnp.logical_not(first))
    def _():
        for n in range(count):
            down_copy(n).start()

    for n in range(count):
        up_copy(n).start()
    x_copy.wait()
    gain_copy.wait()
    gain_row = gain_here[...]
    for kk in range(2):

        def prepare(p, carry):
            raw = x_here[(core + kk) % 2, p]
            scaled, stats = norm_stats(raw, gain_row)
            rows = pl.ds(pl.multiple_of((kk * 4 + p) * 32, 32), 32)
            xs[rows, :] = jnp.where(first, scaled, raw)
            put_stats(outs[kk], pl.multiple_of(p * 32, 32), columns, stats, row_at)
            return carry

        lax.fori_loop(0, 4, prepare, 0)
    xs[pl.ds(2 * half, EXTRA), :] = placed(pieces32(gain_row), row_at).astype(bf16)
    for to in outs[:2]:
        to[pl.ds(half, EXTRA), pl.ds(columns, LANES)] = jnp.zeros((EXTRA, LANES), to.dtype)

    for n in range(count):
        own, other = outs[n // 2 * 2 : n // 2 * 2 + 2]
        columns_at = pl.ds(n % 2 * wide, wide)

        def store(result, extra):
            store_halves(own, other, columns_at, result)
            rows = placed(pieces32(jnp.sum(extra, axis=0, keepdims=True)), row_at)
            own[pl.ds(half, EXTRA), columns_at] = rows
            other[pl.ds(half, EXTRA), columns_at] = rows.astype(bf16)

        @pl.when(first)
        def _():
            up_copy(n).wait()
            result = mul(xs[...], up_tiles[n], NN)
            store(result[: 2 * half], result[2 * half :])

        @pl.when(jnp.logical_not(first))
        def _():
            down_copy(n).wait()
            result = mul(xs[pl.ds(0, 2 * half), :], down_tiles[n], NT)
            up_copy(n).wait()
            store(result, mul(xs[pl.ds(2 * half, EXTRA), :], up_tiles[n], NN))


def start_in(at, x, gain, up, down):
    width, hidden = up.shape
    wide, count = hidden // 4, 4
    rows = 128 + EXTRA
    outs = pl.pallas_call(
        start_kernel,
        out_shape=half_shapes(rows, hidden // 2 + LANES) + half_shapes(rows, hidden // 2),
        in_specs=[SMEM] + [HBM] * 4,
        out_specs=[VMEM] * 4,
        scratch_shapes=[
            pltpu.VMEM((256 + EXTRA, width), bf16),
            pltpu.VMEM(x.shape, bf16),
            pltpu.VMEM(gain.shape, f32),
            pltpu.VMEM((count, width, wide), bf16),
            pltpu.VMEM((count, wide, width), bf16),
            pltpu.SemaphoreType.DMA((3, count)),
        ],
        compiler_params=pltpu.CompilerParams(vmem_limit_bytes=24 * 1024 * 1024),
        cost_estimate=pl.CostEstimate(
            flops=2 * 256 * width * hidden, bytes_accessed=2 * width * hidden, transcendentals=0
        ),
        name="start_in",
    )(at, *(pltpu.with_memory_space_constraint(v, pltpu.HBM) for v in (x, gain, up, down)))
    return outs[:2], outs[2:]


def up_kernel(at, x, gain, up, *refs):
    outs, (xs, up_tiles, sems) = refs[:4], refs[4:]
    count, _, wide = up_tiles.shape
    columns = outs[2].shape[1]

    def up_copy(n):
        return pltpu.make_async_copy(up.at[:, pl.ds(n * wide, wide)], up_tiles.at[n], sems.at[n])

    for n in range(count):
        up_copy(n).start()
    gain_row = gain[...]
    for kk in range(2):

        def prepare(p, carry):
            scaled, stats = norm_stats(x[(at[1] + kk) % 2 * 4 + p], gain_row)
            xs[pl.ds(pl.multiple_of((kk * 4 + p) * 32, 32), 32), :] = scaled
            put_stats(outs[kk], pl.multiple_of(p * 32, 32), columns, stats, at[2])
            return carry

        lax.fori_loop(0, 4, prepare, 0)
    for n in range(count):
        up_copy(n).wait()
        result = mul(xs[...], up_tiles[n], NN)
        store_halves(*outs[n // 2 * 2 : n // 2 * 2 + 2], pl.ds(n % 2 * wide, wide), result)


def up_in(at, x, gain, up):
    width, hidden = up.shape
    wide, count = hidden // 4, 4
    outs = pl.pallas_call(
        up_kernel,
        out_shape=half_shapes(128, hidden // 2 + LANES) + half_shapes(128, hidden // 2),
        in_specs=[SMEM, VMEM, VMEM, HBM],
        out_specs=[VMEM] * 4,
        scratch_shapes=[
            pltpu.VMEM((256, width), bf16),
            pltpu.VMEM((count, width, wide), bf16),
            pltpu.SemaphoreType.DMA((count,)),
        ],
        compiler_params=pltpu.CompilerParams(vmem_limit_bytes=14 * 1024 * 1024),
        cost_estimate=pl.CostEstimate(
            flops=2 * 256 * width * hidden, bytes_accessed=2 * width * hidden, transcendentals=0
        ),
        name="up_in",
    )(at, x, gain, pltpu.with_memory_space_constraint(up, pltpu.HBM))
    return outs[:2], outs[2:]


def down_back_kernel(part, at, x, down, own, other):
    wide = own.shape[1] // 2
    rows = jnp.concatenate([x[at[1]], x[1 - at[1]]], axis=0)
    for n in range(2):
        result = mul(rows, down[pl.ds((2 * part + n) * wide, wide), :], NT)
        store_halves(own, other, pl.ds(n * wide, wide), result)


def local_call(kernel, shapes, operands, name, flops, nbytes, smem=False, scratch=()):
    specs = [SMEM if smem and i == 0 else VMEM for i in range(len(operands))]
    return pl.pallas_call(
        kernel,
        out_shape=shapes,
        in_specs=specs,
        out_specs=[VMEM] * len(shapes),
        scratch_shapes=list(scratch),
        compiler_params=pltpu.CompilerParams(vmem_limit_bytes=6 * 1024 * 1024),
        cost_estimate=pl.CostEstimate(flops=flops, bytes_accessed=nbytes, transcendentals=0),
        name=name,
    )(*operands)


def half_shapes(rows, columns):
    return [
        jax.ShapeDtypeStruct((rows, columns), f32),
        jax.ShapeDtypeStruct((rows, columns), bf16),
    ]


def down_back_in(at, x, down):
    hidden, width = down.shape
    return [
        local_call(
            functools.partial(down_back_kernel, part),
            half_shapes(128, hidden // 2),
            (at, x.reshape(2, 128, width), down),
            f"down_back_{part}",
            256 * width * hidden,
            width * hidden,
            smem=True,
        )
        for part in range(2)
    ]


def row_out_kernel(mode, at, *refs):
    inputs, rest, (out, xs) = refs[:4], refs[4:-2], refs[-2:]
    first = at[0] == 1
    half, columns = 128, xs.shape[1] // 2
    width = out.shape[-1]
    for i in range(2):
        for j in range(2):
            ref = inputs[2 * i + j]
            xs[pl.ds(i * half, half), pl.ds(j * columns, columns)] = ref[:, pl.ds(0, columns)]

    def terms():
        gain, x = rest[:2]
        for i in range(2):
            early, late = (r[:, pl.ds(columns, LANES)].astype(f32) for r in inputs[2 * i : 2 * i + 2])
            ext = early + late
            first0, second0, first1, second1, mean, inv_std = (
                ext[:, 3 * k : 3 * k + 1] + ext[:, 3 * k + 1 : 3 * k + 2] + ext[:, 3 * k + 2 : 3 * k + 3]
                for k in range(6)
            )
            for p in range(4):
                pick = slice(p * 32, p * 32 + 32)
                yield (
                    i * 4 + p,
                    gain,
                    x.at[(at[1] + i) % 2, p] if mode == 2 else x.at[(at[1] + i) % 2 * 4 + p],
                    (first0 + first1)[pick],
                    (second0 + second1)[pick],
                    mean[pick],
                    inv_std[pick],
                )

    def steps(weight, dims, back):
        saved = list(terms()) if back else []

        def step(n, carry):
            at_n = pl.ds(pl.multiple_of(n * 512, 512), 512)
            tile = weight[:, at_n] if dims is NN else weight[at_n, :]
            result = mul(xs[...], tile, dims)
            if not back:
                for k in range(8):
                    out[(k + 4 * at[1]) % 8, :, at_n] = result[k * 32 : k * 32 + 32].astype(bf16)
            for k, gain, x, first_sum, second_sum, mean, inv_std in saved:
                grad = result[k * 32 : k * 32 + 32] * gain[:, at_n]
                normed = (x[:, at_n].astype(f32) - mean) * inv_std
                out[(k + 4 * at[1]) % 8, :, at_n] = (inv_std * (grad - first_sum - normed * second_sum)).astype(bf16)
            return carry

        lax.fori_loop(0, width // 512, step, 0)

    if mode == 0:
        steps(rest[0], NN, False)
    elif mode == 1:
        steps(rest[2], NT, True)
    else:
        pl.when(first)(lambda: steps(rest[2], NT, True))
        pl.when(jnp.logical_not(first))(lambda: steps(rest[3], NN, False))


def row_out(mode, at, mine, others, rest):
    hidden, width = max(rest[-1].shape), min(rest[-1].shape)
    (out,) = local_call(
        functools.partial(row_out_kernel, mode),
        [jax.ShapeDtypeStruct((8, 32, width), bf16)],
        (at, *mine, *others, *rest),
        f"row_out_{mode}",
        2 * 256 * width * hidden,
        2 * width * hidden,
        smem=True,
        scratch=[pltpu.VMEM((256, hidden), bf16)],
    )
    return out


MEAN, INV = 0, 1
COMBOS = ((0, 0), (0, 1), (1, 0), (0, 2), (1, 1), (2, 0))


def act_kernel(mode, part, at, *refs):
    refs = list(refs)
    first = at[0] == 1
    sums = [(refs.pop(0), refs.pop(0)) for _ in range(2)]
    stats = refs.pop(0) if mode == 2 or part else None
    factors = refs.pop(0) if mode != 2 and part else None
    gains = refs.pop(0) if mode == 1 else None
    totals = refs.pop(0) if mode else None
    saved = refs.pop(0) if mode else None
    hidden = refs.pop(0) if mode == 2 else None
    chunk = refs.pop(0)
    saved_out = refs.pop(0) if mode == 0 else None
    gains_out = refs.pop(0) if mode == 0 else None
    totals_out = refs.pop(0) if mode == 0 else None
    hidden_out = refs.pop(0) if mode == 1 else None
    stats_out = refs.pop(0) if mode != 2 and part == 0 else None
    factors_out = refs.pop(0) if mode != 2 and part == 0 else None
    shifted = refs.pop(0) if mode != 2 else None
    wide = 1024
    total_width = 8192
    lane = lax.broadcasted_iota(jnp.int32, (1, LANES), 1)
    if mode == 0:
        gains = gains_out
        gains[...] = jnp.zeros_like(gains)
        for q, (held, arrived) in enumerate(sums):
            columns = pl.ds(q * wide, wide)
            extra = held[pl.ds(128, EXTRA), pl.ds(0, wide)] + arrived[pl.ds(128, EXTRA), pl.ds(0, wide)].astype(f32)
            rows8 = jnp.concatenate(
                [jnp.sum(extra[3 * r : 3 * r + 3], axis=0, keepdims=True) for r in range(8)], axis=0
            )
            totals_out[:, columns] = jnp.sum(rows8, axis=0, keepdims=True)
            split = pieces32(rows8)
            stacked = jnp.concatenate([split[j] for _, j in COMBOS], axis=0)
            gains[pl.ds(0, 48), columns] = stacked.astype(bf16)
    if stats_out is not None:
        stats = stats_out
        held, arrived = sums[1]
        ext = held[pl.ds(0, 128), pl.ds(wide, LANES)] + arrived[pl.ds(0, 128), pl.ds(wide, LANES)].astype(f32)
        means = [sum(ext[:, 8 * k + r : 8 * k + r + 1] for k in range(3)) for r in range(8)]
        mean = sum(means) / 8
        shifts = [value - mean for value in means]
        squares = jnp.sum(jnp.where((lane >= 24) & (lane < 48), ext, 0.0), axis=1, keepdims=True)
        variance = (squares + wide * sum(value * value for value in shifts)) / total_width
        inv_std = lax.rsqrt(variance + epsilon)
        if mode == 0:
            inv_std = jnp.where(first, inv_std, 1.0)
            shifts = [jnp.where(first, value, 0.0) for value in shifts]
        out = jnp.where(lane == MEAN, mean, 0.0) + jnp.where(lane == INV, inv_std, 0.0)
        stats[...] = out
        placed_at = jnp.zeros((128, LANES), f32)
        for r, value in enumerate(shifts):
            split = pieces32(value)
            for k, (j, _) in enumerate(COMBOS):
                placed_at = placed_at + jnp.where(lane == 8 * k + r, split[j], 0.0)
        factors_out[...] = placed_at.astype(bf16)
        factors = factors_out
    if mode != 2:
        for q in range(4):
            columns = pl.ds(q * 512, 512)
            shifted[:, columns] = mul(factors[...], gains[:, columns], NN)

    size, span = 16, 512

    def block(i, carry):
        rows = pl.ds(pl.multiple_of(i * size, size), size)
        here = stats[rows, :]
        mean, inv_std = here[:, MEAN : MEAN + 1], here[:, INV : INV + 1]
        firsts = jnp.zeros((size, span), f32)
        seconds = jnp.zeros((size, span), f32)
        for n in range(2 * wide // span):
            columns = pl.ds(n * span, span)
            held, arrived = sums[n * span // wide]
            inner = pl.ds(n * span % wide, span)
            value = held[rows, inner] + arrived[rows, inner].astype(f32)
            if mode != 2:
                value = inv_std * (value + shifted[rows, columns])
            pre = saved[rows, columns] if mode == 2 else value
            if mode == 0:
                saved_out[rows, columns] = pre
                chunk[rows, columns] = gelu_value(pre).astype(bf16)
                continue
            tangent = gelu_tangent(pre)
            slope = 0.5 * (1.0 + tangent) + 0.5 * pre * (1.0 - tangent * tangent) * gelu_coeff * (
                1.0 + 3.0 * 0.044715 * pre * pre
            )
            grad = (value if mode == 2 else saved[rows, columns]) * slope
            grad_sent = grad.astype(bf16)
            if mode == 1:
                hidden_out[rows, columns] = (0.5 * pre * (1.0 + tangent)).astype(bf16)
                chunk[rows, columns] = grad_sent
            else:
                chunk[rows, columns] = jnp.where(first, grad_sent, hidden[rows, columns])
            grad = grad_sent.astype(f32)
            firsts = firsts + grad * totals[:, columns]
            seconds = seconds + grad * pre
        if mode:
            values = [
                jnp.sum(v, axis=1, keepdims=True) / total_width for v in (firsts, seconds)
            ] + ([mean, inv_std] if part else [])
            ext = jnp.zeros((size, LANES), f32)
            spot = 6 * part
            for value in values:
                for piece in pieces32(value):
                    ext = ext + jnp.where(lane == spot, piece, 0.0)
                    spot += 1
            chunk[rows, pl.ds(2 * wide, LANES)] = ext.astype(bf16)
        return carry

    lax.fori_loop(0, 128 // size, block, 0)


def act(mode, part, at, sums, stats, gains, saved, hidden):
    wide = 2048
    operands = [at] + [ref for pair in sums for ref in pair]
    if mode == 2 or part:
        operands.append(stats[0])
    if mode != 2 and part:
        operands.append(stats[1])
    if mode == 1:
        operands.append(gains[0])
    if mode:
        operands += [gains[1], saved]
    if mode == 2:
        operands.append(hidden)
    shapes = [jax.ShapeDtypeStruct((128, wide + (LANES if mode else 0)), bf16)]
    if mode == 0:
        shapes.append(jax.ShapeDtypeStruct((128, wide), f32))
        shapes.append(jax.ShapeDtypeStruct((LANES, wide), bf16))
        shapes.append(jax.ShapeDtypeStruct((1, wide), f32))
    if mode == 1:
        shapes.append(jax.ShapeDtypeStruct((128, wide), bf16))
    if mode != 2 and part == 0:
        shapes.append(jax.ShapeDtypeStruct((128, LANES), f32))
        shapes.append(jax.ShapeDtypeStruct((128, LANES), bf16))
    return local_call(
        functools.partial(act_kernel, mode, part),
        shapes,
        operands,
        f"act_{mode}_{part}",
        40 * 128 * wide,
        16 * 128 * wide,
        smem=True,
        scratch=[pltpu.VMEM((128, wide), f32)] if mode != 2 else (),
    )


def finish_kernel(parts, base, out):
    total = base[...].astype(f32)
    for k in range(8):
        total = total + parts[k].astype(f32)
    total = total.astype(bf16)
    if len(out.shape) == 2:
        out[...] = total
    else:
        for k in range(8):
            out[k] = total


def finish(parts, base, copies):
    block, width = base.shape
    (out,) = local_call(
        finish_kernel,
        [jax.ShapeDtypeStruct((8, block, width) if copies else base.shape, bf16)],
        (parts, base),
        "finish",
        8 * block * width,
        20 * block * width,
    )
    return out


def permuted(array, axis, mapping):
    return lax.ppermute(array, axis, [(i, mapping(i)) for i in range(lax.axis_size(axis))])


def body(section_feeds, norm_gain, up_weight, down_weight):
    up = up_weight[0]
    down = down_weight[0]
    gain = norm_gain
    width, hidden = up.shape
    micro, rows = section_feeds.shape[1], section_feeds.shape[2]
    rsize, tsize = lax.axis_size("row"), lax.axis_size("tp")
    tokens = micro * rows
    block = tokens // tsize
    is_first = lax.axis_index("section") == 0
    row_at = lax.axis_index("row")
    tp_at = lax.axis_index("tp")
    core = row_at % 2
    at = jnp.stack([is_first.astype(jnp.int32), core, row_at])

    def pair(i):
        return i ^ 1

    def near(i):
        return i ^ 2

    def far(i):
        return i ^ 6

    def row_sum(halves):
        sums = []
        for own, other in halves:
            arrived = permuted(other, "row", pair)
            for columns in (slice(0, hidden // 4), slice(hidden // 4, None)):
                sums.append(own[:, columns] + arrived[:, columns].astype(f32))
        ways = (near, far, near, far)
        arrived = [permuted(h.astype(bf16), "row", way) for h, way in zip(sums, ways)]
        sums = [h + r.astype(f32) for h, r in zip(sums, arrived)]
        ways = (far, near, far, near)
        arrived = [permuted(h.astype(bf16), "row", way) for h, way in zip(sums, ways)]
        quarters = list(zip(sums, arrived))
        return quarters[:2], quarters[2:]

    def swapped(chunks):
        return chunks, [permuted(chunk, "row", pair) for chunk in chunks]

    def along_tp(part):
        return lax.all_to_all(part, "tp", 0, 0)

    blocks = rows // block
    feeds = section_feeds[0].reshape(micro, blocks, block, width)
    own_feed = lax.dynamic_index_in_dim(
        feeds.reshape(tsize, block, width), tp_at, 0, keepdims=False
    )
    early, late = row_sum(start_in(at, feeds, gain, up, down))
    chunk0, saved00, *gains0, stats, factors = act(0, 0, at, early, None, None, None, None)
    stats0 = (stats, factors)
    chunk1, saved01, *gains1 = act(0, 1, at, late, stats0, None, None, None)
    chunks, saved0, gain_rows = [chunk0, chunk1], [saved00, saved01], [gains0, gains1]
    parts = along_tp(row_out(0, at, *swapped(chunks), (down,)))
    middle = lax.ppermute(finish(parts, own_feed, False), "section", [(0, 1)])
    middles = along_tp(jnp.broadcast_to(middle[None], (tsize,) + middle.shape))

    early, late = row_sum(up_in(at, middles, gain, up))
    chunk0, hidden0, *stats1 = act(1, 0, at, early, None, gain_rows[0], saved0[0], None)
    chunk1, hidden1 = act(1, 1, at, late, stats1, gain_rows[1], saved0[1], None)
    chunks = [chunk0, chunk1]
    parts = along_tp(row_out(1, at, *swapped(chunks), (gain, middles, up)))
    back = lax.ppermute(finish(parts, own_feed, False), "section", [(1, 0)])
    backs = along_tp(jnp.broadcast_to(back[None], (tsize,) + back.shape))

    early, late = row_sum(down_back_in(at, backs, down))
    chunks = []
    for part, sums in enumerate((early, late)):
        kept = (hidden0, hidden1)[part]
        (chunk,) = act(2, part, at, sums, stats0, gain_rows[part], saved0[part], kept)
        chunks.append(chunk)
    parts = along_tp(row_out(2, at, *swapped(chunks), (gain, feeds, up, down)))
    base = jnp.where(is_first, back, middle)
    return along_tp(finish(parts, base, True)).reshape(section_feeds.shape)


def solution(mesh):
    placed = (
        P("section", None, None, "row"),
        P("section", "row"),
        P("section", "row", "tp"),
        P("section", "tp", "row"),
    )
    return jax.shard_map(
        body, mesh=mesh, in_specs=placed, out_specs=P("section", None, None, "row"), check_vma=False
    )
```

```python
import functools

import jax
import jax.numpy as jnp
from jax import lax
from jax.experimental import pallas as pl
from jax.experimental.pallas import tpu as pltpu
from jax.sharding import PartitionSpec as P

epsilon = 1e-05
gelu_coeff = 0.7978845608028654
LANES = 128
EXTRA = 32
f32 = jnp.float32
bf16 = jnp.bfloat16
NN = (((1,), (0,)), ((), ()))
NT = (((1,), (1,)), ((), ()))
HBM = pl.BlockSpec(memory_space=pltpu.HBM)
VMEM = pl.BlockSpec(memory_space=pltpu.VMEM)
SMEM = pl.BlockSpec(memory_space=pltpu.SMEM)


def gelu_gate(inputs, square):
    inner = inputs * (gelu_coeff + gelu_coeff * 0.044715 * square)
    return 0.5 + 0.5 * jnp.tanh(inner)


def gelu_slope(inputs, square, gate):
    rise = inputs * (2.0 * gelu_coeff + 6.0 * gelu_coeff * 0.044715 * square)
    return gate * (1.0 + (1.0 - gate) * rise)


def pieces(value):
    high = value.astype(bf16)
    rest = value - high.astype(f32)
    middle = rest.astype(bf16)
    low = (rest - middle.astype(f32)).astype(bf16)
    return high, middle, low


def pieces32(value):
    return tuple(part.astype(f32) for part in pieces(value))


def mul(a, b, dims):
    return lax.dot_general(a, b, dims, preferred_element_type=f32)


def norm_stats(raw, gain_row):
    values = raw.astype(f32)
    mean = jnp.sum(values, axis=1, keepdims=True) / values.shape[1]
    centred = values - mean
    squares = jnp.sum(centred * centred, axis=1, keepdims=True)
    return (centred * gain_row).astype(bf16), pieces32(mean) + pieces32(squares)


def put_stats(to, start, lanes, stats, row_at):
    lane = lax.broadcasted_iota(jnp.int32, (1, LANES), 1)
    ext = jnp.zeros((stats[0].shape[0], LANES), f32)
    for i, part in enumerate(stats):
        ext = ext + jnp.where(lane == i * 8 + row_at, part, 0.0)
    to[pl.ds(start, ext.shape[0]), pl.ds(lanes, LANES)] = ext.astype(to.dtype)


def placed(parts, row_at):
    spot = lax.broadcasted_iota(jnp.int32, (EXTRA, 1), 0)
    return sum(jnp.where(spot == 3 * row_at + j, part, 0.0) for j, part in enumerate(parts))


def store_halves(own, other, columns, result):
    half = result.shape[0] // 2
    own[pl.ds(0, half), columns] = result[:half]
    other[pl.ds(0, half), columns] = result[half:].astype(bf16)


def start_kernel(at, x, gain, up, down, *refs):
    outs, (xs, x_here, gain_here, up_tiles, down_tiles, sems) = refs[:4], refs[4:]
    first = at[0] == 1
    core, row_at = at[1], at[2]
    count, _, wide = up_tiles.shape
    half = outs[0].shape[0] - EXTRA
    columns = outs[2].shape[1]

    def up_copy(n):
        return pltpu.make_async_copy(up.at[:, pl.ds(n * wide, wide)], up_tiles.at[n], sems.at[0, n])

    def down_copy(n):
        return pltpu.make_async_copy(down.at[pl.ds(n * wide, wide)], down_tiles.at[n], sems.at[1, n])

    x_copy = pltpu.make_async_copy(x, x_here, sems.at[2, 0])
    gain_copy = pltpu.make_async_copy(gain, gain_here, sems.at[2, 1])
    x_copy.start()
    gain_copy.start()

    @pl.when(jnp.logical_not(first))
    def _():
        for n in range(count):
            down_copy(n).start()

    for n in range(count):
        up_copy(n).start()
    x_copy.wait()
    gain_copy.wait()
    gain_row = gain_here[...]
    for kk in range(2):

        def prepare(p, carry):
            raw = x_here[(core + kk) % 2, p]
            scaled, stats = norm_stats(raw, gain_row)
            rows = pl.ds(pl.multiple_of((kk * 4 + p) * 32, 32), 32)
            xs[rows, :] = jnp.where(first, scaled, raw)
            put_stats(outs[kk], pl.multiple_of(p * 32, 32), columns, stats, row_at)
            return carry

        lax.fori_loop(0, 4, prepare, 0)
    xs[pl.ds(2 * half, EXTRA), :] = placed(pieces32(gain_row), row_at).astype(bf16)
    for to in outs[:2]:
        to[pl.ds(half, EXTRA), pl.ds(columns, LANES)] = jnp.zeros((EXTRA, LANES), to.dtype)

    for n in range(count):
        own, other = outs[n // 2 * 2 : n // 2 * 2 + 2]
        columns_at = pl.ds(n % 2 * wide, wide)

        def store(result, extra):
            store_halves(own, other, columns_at, result)
            rows = placed(pieces32(jnp.sum(extra, axis=0, keepdims=True)), row_at)
            own[pl.ds(half, EXTRA), columns_at] = rows
            other[pl.ds(half, EXTRA), columns_at] = rows.astype(bf16)

        @pl.when(first)
        def _():
            up_copy(n).wait()
            result = mul(xs[...], up_tiles[n], NN)
            store(result[: 2 * half], result[2 * half :])

        @pl.when(jnp.logical_not(first))
        def _():
            down_copy(n).wait()
            result = mul(xs[pl.ds(0, 2 * half), :], down_tiles[n], NT)
            up_copy(n).wait()
            store(result, mul(xs[pl.ds(2 * half, EXTRA), :], up_tiles[n], NN))


def start_in(at, x, gain, up, down):
    width, hidden = up.shape
    wide, count = hidden // 4, 4
    rows = 128 + EXTRA
    outs = pl.pallas_call(
        start_kernel,
        out_shape=half_shapes(rows, hidden // 2 + LANES) + half_shapes(rows, hidden // 2),
        in_specs=[SMEM] + [HBM] * 4,
        out_specs=[VMEM] * 4,
        scratch_shapes=[
            pltpu.VMEM((256 + EXTRA, width), bf16),
            pltpu.VMEM(x.shape, bf16),
            pltpu.VMEM(gain.shape, f32),
            pltpu.VMEM((count, width, wide), bf16),
            pltpu.VMEM((count, wide, width), bf16),
            pltpu.SemaphoreType.DMA((3, count)),
        ],
        compiler_params=pltpu.CompilerParams(vmem_limit_bytes=24 * 1024 * 1024),
        cost_estimate=pl.CostEstimate(
            flops=2 * 256 * width * hidden, bytes_accessed=2 * width * hidden, transcendentals=0
        ),
        name="start_in",
    )(at, *(pltpu.with_memory_space_constraint(v, pltpu.HBM) for v in (x, gain, up, down)))
    return outs[:2], outs[2:]


def up_kernel(at, x, gain, up, *refs):
    outs, (xs, up_tiles, sems) = refs[:4], refs[4:]
    count, _, wide = up_tiles.shape
    columns = outs[2].shape[1]

    def up_copy(n):
        return pltpu.make_async_copy(up.at[:, pl.ds(n * wide, wide)], up_tiles.at[n], sems.at[n])

    for n in range(count):
        up_copy(n).start()
    gain_row = gain[...]
    for kk in range(2):

        def prepare(p, carry):
            scaled, stats = norm_stats(x[(at[1] + kk) % 2 * 4 + p], gain_row)
            xs[pl.ds(pl.multiple_of((kk * 4 + p) * 32, 32), 32), :] = scaled
            put_stats(outs[kk], pl.multiple_of(p * 32, 32), columns, stats, at[2])
            return carry

        lax.fori_loop(0, 4, prepare, 0)
    for n in range(count):
        up_copy(n).wait()
        result = mul(xs[...], up_tiles[n], NN)
        store_halves(*outs[n // 2 * 2 : n // 2 * 2 + 2], pl.ds(n % 2 * wide, wide), result)


def up_in(at, x, gain, up):
    width, hidden = up.shape
    wide, count = hidden // 4, 4
    outs = pl.pallas_call(
        up_kernel,
        out_shape=half_shapes(128, hidden // 2 + LANES) + half_shapes(128, hidden // 2),
        in_specs=[SMEM, VMEM, VMEM, HBM],
        out_specs=[VMEM] * 4,
        scratch_shapes=[
            pltpu.VMEM((256, width), bf16),
            pltpu.VMEM((count, width, wide), bf16),
            pltpu.SemaphoreType.DMA((count,)),
        ],
        compiler_params=pltpu.CompilerParams(vmem_limit_bytes=14 * 1024 * 1024),
        cost_estimate=pl.CostEstimate(
            flops=2 * 256 * width * hidden, bytes_accessed=2 * width * hidden, transcendentals=0
        ),
        name="up_in",
    )(at, x, gain, pltpu.with_memory_space_constraint(up, pltpu.HBM))
    return outs[:2], outs[2:]


def down_back_kernel(part, at, x, down, own, other):
    wide = own.shape[1] // 2
    half = own.shape[0]
    for n in range(2):
        result = mul(x[...], down[pl.ds((2 * part + n) * wide, wide), :], NT)
        low, high = result[:half], result[half:]
        columns = pl.ds(n * wide, wide)
        own[:, columns] = jnp.where(at[1] == 0, low, high)
        other[:, columns] = jnp.where(at[1] == 0, high, low).astype(bf16)


def local_call(kernel, shapes, operands, name, flops, nbytes, smem=False, scratch=()):
    specs = [SMEM if smem and i == 0 else VMEM for i in range(len(operands))]
    return pl.pallas_call(
        kernel,
        out_shape=shapes,
        in_specs=specs,
        out_specs=[VMEM] * len(shapes),
        scratch_shapes=list(scratch),
        compiler_params=pltpu.CompilerParams(vmem_limit_bytes=6 * 1024 * 1024),
        cost_estimate=pl.CostEstimate(flops=flops, bytes_accessed=nbytes, transcendentals=0),
        name=name,
    )(*operands)


def half_shapes(rows, columns):
    return [
        jax.ShapeDtypeStruct((rows, columns), f32),
        jax.ShapeDtypeStruct((rows, columns), bf16),
    ]


def down_back_in(at, x, down):
    hidden, width = down.shape
    return [
        local_call(
            functools.partial(down_back_kernel, part),
            half_shapes(128, hidden // 2),
            (at, x.reshape(256, width), down),
            f"down_back_{part}",
            256 * width * hidden,
            width * hidden,
            smem=True,
        )
        for part in range(2)
    ]


def row_out_kernel(mode, at, *refs):
    inputs, rest, (out, xs) = refs[:4], refs[4:-2], refs[-2:]
    first = at[0] == 1
    half, columns = 128, xs.shape[1] // 2
    width = out.shape[-1]
    if mode:
        for i in range(2):
            for j in range(2):
                ref = inputs[2 * i + j]
                xs[pl.ds(i * half, half), pl.ds(j * columns, columns)] = ref[:, pl.ds(0, columns)]

    def direct(weight):
        def step(n, carry):
            at_n = pl.ds(pl.multiple_of(n * 512, 512), 512)
            for i in range(2):
                result = mul(inputs[2 * i][...], weight[pl.ds(0, columns), at_n], NN)
                result = result + mul(inputs[2 * i + 1][...], weight[pl.ds(columns, columns), at_n], NN)
                for k in range(4):
                    out[(4 * i + k + 4 * at[1]) % 8, :, at_n] = result[k * 32 : k * 32 + 32].astype(bf16)
            return carry

        lax.fori_loop(0, width // 512, step, 0)

    def terms():
        gain, x = rest[:2]
        for i in range(2):
            early, late = (r[:, pl.ds(columns, LANES)].astype(f32) for r in inputs[2 * i : 2 * i + 2])
            ext = early + late
            first0, second0, first1, second1, mean, inv_std = (
                ext[:, 3 * k : 3 * k + 1] + ext[:, 3 * k + 1 : 3 * k + 2] + ext[:, 3 * k + 2 : 3 * k + 3]
                for k in range(6)
            )
            for p in range(4):
                pick = slice(p * 32, p * 32 + 32)
                yield (
                    i * 4 + p,
                    gain,
                    x.at[(at[1] + i) % 2, p] if mode == 2 else x.at[(at[1] + i) % 2 * 4 + p],
                    (first0 + first1)[pick],
                    (second0 + second1)[pick],
                    mean[pick],
                    inv_std[pick],
                )

    def steps(weight, dims, back):
        saved = list(terms()) if back else []

        def step(n, carry):
            at_n = pl.ds(pl.multiple_of(n * 512, 512), 512)
            tile = weight[:, at_n] if dims is NN else weight[at_n, :]
            result = mul(xs[...], tile, dims)
            if not back:
                for k in range(8):
                    out[(k + 4 * at[1]) % 8, :, at_n] = result[k * 32 : k * 32 + 32].astype(bf16)
            for k, gain, x, first_sum, second_sum, mean, inv_std in saved:
                grad = result[k * 32 : k * 32 + 32] * gain[:, at_n]
                normed = (x[:, at_n].astype(f32) - mean) * inv_std
                out[(k + 4 * at[1]) % 8, :, at_n] = (inv_std * (grad - first_sum - normed * second_sum)).astype(bf16)
            return carry

        lax.fori_loop(0, width // 512, step, 0)

    if mode == 0:
        pl.when(first)(lambda: direct(rest[0]))
    elif mode == 1:
        steps(rest[2], NT, True)
    else:
        pl.when(first)(lambda: steps(rest[2], NT, True))
        pl.when(jnp.logical_not(first))(lambda: steps(rest[3], NN, False))


def row_out(mode, at, mine, others, rest):
    hidden, width = max(rest[-1].shape), min(rest[-1].shape)
    (out,) = local_call(
        functools.partial(row_out_kernel, mode),
        [jax.ShapeDtypeStruct((8, 32, width), bf16)],
        (at, *mine, *others, *rest),
        f"row_out_{mode}",
        2 * 256 * width * hidden,
        2 * width * hidden,
        smem=True,
        scratch=[pltpu.VMEM((256, hidden), bf16)],
    )
    return out


MEAN, INV = 0, 1
COMBOS = ((0, 0), (0, 1), (1, 0), (0, 2), (1, 1), (2, 0))


def act_kernel(mode, part, at, *refs):
    refs = list(refs)
    first = at[0] == 1
    sums = [(refs.pop(0), refs.pop(0)) for _ in range(2)]
    stats = refs.pop(0) if mode == 2 or part else None
    factors = refs.pop(0) if mode != 2 and part else None
    gains = refs.pop(0) if mode == 1 else None
    totals = refs.pop(0) if mode else None
    saved = refs.pop(0) if mode else None
    hidden = refs.pop(0) if mode == 2 else None
    chunk = refs.pop(0)
    saved_out = refs.pop(0) if mode == 0 else None
    gains_out = refs.pop(0) if mode == 0 else None
    totals_out = refs.pop(0) if mode == 0 else None
    hidden_out = refs.pop(0) if mode == 1 else None
    stats_out = refs.pop(0) if mode != 2 and part == 0 else None
    factors_out = refs.pop(0) if mode != 2 and part == 0 else None
    shifted = refs.pop(0) if mode != 2 else None
    wide = 1024
    total_width = 8192
    lane = lax.broadcasted_iota(jnp.int32, (1, LANES), 1)
    if mode == 0:
        for q, (held, arrived) in enumerate(sums):
            columns = pl.ds(q * wide, wide)
            extra = held[pl.ds(128, EXTRA), pl.ds(0, wide)] + arrived[pl.ds(128, EXTRA), pl.ds(0, wide)].astype(f32)
            rows8 = jnp.concatenate(
                [jnp.sum(extra[3 * r : 3 * r + 3], axis=0, keepdims=True) for r in range(8)], axis=0
            )
            gains_out[:, columns] = rows8
            totals_out[:, columns] = jnp.sum(rows8, axis=0, keepdims=True)
        gains = gains_out
    if stats_out is not None:
        stats = stats_out
        held, arrived = sums[1]
        ext = held[pl.ds(0, 128), pl.ds(wide, LANES)] + arrived[pl.ds(0, 128), pl.ds(wide, LANES)].astype(f32)
        means = [sum(ext[:, 8 * k + r : 8 * k + r + 1] for k in range(3)) for r in range(8)]
        mean = sum(means) / 8
        shifts = [value - mean for value in means]
        squares = jnp.sum(jnp.where((lane >= 24) & (lane < 48), ext, 0.0), axis=1, keepdims=True)
        variance = (squares + wide * sum(value * value for value in shifts)) / total_width
        inv_std = lax.rsqrt(variance + epsilon)
        if mode == 0:
            inv_std = jnp.where(first, inv_std, 1.0)
            shifts = [jnp.where(first, value, 0.0) for value in shifts]
        out = jnp.where(lane == MEAN, mean, 0.0) + jnp.where(lane == INV, inv_std, 0.0)
        stats[...] = out
        placed_at = jnp.zeros((128, LANES), f32)
        for r, value in enumerate(shifts):
            split = pieces32(value)
            for k, (j, _) in enumerate(COMBOS):
                placed_at = placed_at + jnp.where(lane == 8 * k + r, split[j], 0.0)
        factors_out[...] = placed_at.astype(bf16)
        factors = factors_out
    if mode != 2:
        for q in range(4):
            columns = pl.ds(q * 512, 512)
            split = pieces32(gains[:, columns])
            zeros = jnp.zeros((LANES - 8 * len(COMBOS), 512), f32)
            stacked = jnp.concatenate([split[j] for _, j in COMBOS] + [zeros], axis=0)
            shifted[:, columns] = mul(factors[...], stacked.astype(bf16), NN)

    size, span = 16, 512

    def block(i, carry):
        rows = pl.ds(pl.multiple_of(i * size, size), size)
        here = stats[rows, :]
        mean, inv_std = here[:, MEAN : MEAN + 1], here[:, INV : INV + 1]
        firsts = jnp.zeros((size, span), f32)
        seconds = jnp.zeros((size, span), f32)
        for n in range(2 * wide // span):
            columns = pl.ds(n * span, span)
            held, arrived = sums[n * span // wide]
            inner = pl.ds(n * span % wide, span)
            value = held[rows, inner] + arrived[rows, inner].astype(f32)
            if mode != 2:
                value = inv_std * (value + shifted[rows, columns])
            pre = saved[rows, columns] if mode == 2 else value
            square = pre * pre
            gate = gelu_gate(pre, square)
            if mode == 0:
                saved_out[rows, columns] = pre
                chunk[rows, columns] = (pre * gate).astype(bf16)
                continue
            slope = gelu_slope(pre, square, gate)
            grad = (value if mode == 2 else saved[rows, columns]) * slope
            grad_sent = grad.astype(bf16)
            if mode == 1:
                hidden_out[rows, columns] = (pre * gate).astype(bf16)
                chunk[rows, columns] = grad_sent
            else:
                chunk[rows, columns] = jnp.where(first, grad_sent, hidden[rows, columns])
            grad = grad_sent.astype(f32)
            firsts = firsts + grad * totals[:, columns]
            seconds = seconds + grad * pre
        if mode:
            values = [
                jnp.sum(v, axis=1, keepdims=True) / total_width for v in (firsts, seconds)
            ] + ([mean, inv_std] if part else [])
            ext = jnp.zeros((size, LANES), f32)
            spot = 6 * part
            for value in values:
                for piece in pieces32(value):
                    ext = ext + jnp.where(lane == spot, piece, 0.0)
                    spot += 1
            chunk[rows, pl.ds(2 * wide, LANES)] = ext.astype(bf16)
        return carry

    lax.fori_loop(0, 128 // size, block, 0)


def act(mode, part, at, sums, stats, gains, saved, hidden):
    wide = 2048
    operands = [at] + [ref for pair in sums for ref in pair]
    if mode == 2 or part:
        operands.append(stats[0])
    if mode != 2 and part:
        operands.append(stats[1])
    if mode == 1:
        operands.append(gains[0])
    if mode:
        operands += [gains[1], saved]
    if mode == 2:
        operands.append(hidden)
    shapes = [jax.ShapeDtypeStruct((128, wide + (LANES if mode else 0)), bf16)]
    if mode == 0:
        shapes.append(jax.ShapeDtypeStruct((128, wide), f32))
        shapes.append(jax.ShapeDtypeStruct((8, wide), f32))
        shapes.append(jax.ShapeDtypeStruct((1, wide), f32))
    if mode == 1:
        shapes.append(jax.ShapeDtypeStruct((128, wide), bf16))
    if mode != 2 and part == 0:
        shapes.append(jax.ShapeDtypeStruct((128, LANES), f32))
        shapes.append(jax.ShapeDtypeStruct((128, LANES), bf16))
    return local_call(
        functools.partial(act_kernel, mode, part),
        shapes,
        operands,
        f"act_{mode}_{part}",
        40 * 128 * wide,
        16 * 128 * wide,
        smem=True,
        scratch=[pltpu.VMEM((128, wide), f32)] if mode != 2 else (),
    )


def finish_kernel(parts, base, out):
    total = base[...].astype(f32)
    for k in range(8):
        total = total + parts[k].astype(f32)
    total = total.astype(bf16)
    if len(out.shape) == 2:
        out[...] = total
    else:
        for k in range(8):
            out[k] = total


def finish(parts, base, copies):
    block, width = base.shape
    (out,) = local_call(
        finish_kernel,
        [jax.ShapeDtypeStruct((8, block, width) if copies else base.shape, bf16)],
        (parts, base),
        "finish",
        8 * block * width,
        20 * block * width,
    )
    return out


def permuted(array, axis, mapping):
    return lax.ppermute(array, axis, [(i, mapping(i)) for i in range(lax.axis_size(axis))])


def body(section_feeds, norm_gain, up_weight, down_weight):
    up = up_weight[0]
    down = down_weight[0]
    gain = norm_gain
    width, hidden = up.shape
    micro, rows = section_feeds.shape[1], section_feeds.shape[2]
    rsize, tsize = lax.axis_size("row"), lax.axis_size("tp")
    tokens = micro * rows
    block = tokens // tsize
    is_first = lax.axis_index("section") == 0
    row_at = lax.axis_index("row")
    tp_at = lax.axis_index("tp")
    core = row_at % 2
    at = jnp.stack([is_first.astype(jnp.int32), core, row_at])

    def pair(i):
        return i ^ 1

    def near(i):
        return i ^ 2

    def far(i):
        return i ^ 6

    def row_sum(halves):
        sums = []
        for own, other in halves:
            arrived = permuted(other, "row", pair)
            for columns in (slice(0, hidden // 4), slice(hidden // 4, None)):
                sums.append(own[:, columns] + arrived[:, columns].astype(f32))
        ways = (near, far, near, far)
        arrived = [permuted(h.astype(bf16), "row", way) for h, way in zip(sums, ways)]
        sums = [h + r.astype(f32) for h, r in zip(sums, arrived)]
        ways = (far, near, far, near)
        arrived = [permuted(h.astype(bf16), "row", way) for h, way in zip(sums, ways)]
        quarters = list(zip(sums, arrived))
        return quarters[:2], quarters[2:]

    def swapped(chunks):
        return chunks, [permuted(chunk, "row", pair) for chunk in chunks]

    def along_tp(part):
        return lax.all_to_all(part, "tp", 0, 0)

    blocks = rows // block
    feeds = section_feeds[0].reshape(micro, blocks, block, width)
    own_feed = lax.dynamic_index_in_dim(
        feeds.reshape(tsize, block, width), tp_at, 0, keepdims=False
    )
    early, late = row_sum(start_in(at, feeds, gain, up, down))
    chunk0, saved00, *gains0, stats, factors = act(0, 0, at, early, None, None, None, None)
    stats0 = (stats, factors)
    chunk1, saved01, *gains1 = act(0, 1, at, late, stats0, None, None, None)
    chunks, saved0, gain_rows = [chunk0, chunk1], [saved00, saved01], [gains0, gains1]
    parts = along_tp(row_out(0, at, *swapped(chunks), (down,)))
    middle = lax.ppermute(finish(parts, own_feed, False), "section", [(0, 1)])
    middles = along_tp(jnp.broadcast_to(middle[None], (tsize,) + middle.shape))

    early, late = row_sum(up_in(at, middles, gain, up))
    chunk0, hidden0, *stats1 = act(1, 0, at, early, None, gain_rows[0], saved0[0], None)
    chunk1, hidden1 = act(1, 1, at, late, stats1, gain_rows[1], saved0[1], None)
    chunks = [chunk0, chunk1]
    parts = along_tp(row_out(1, at, *swapped(chunks), (gain, middles, up)))
    back = lax.ppermute(finish(parts, own_feed, False), "section", [(1, 0)])
    backs = along_tp(jnp.broadcast_to(back[None], (tsize,) + back.shape))

    early, late = row_sum(down_back_in(at, backs, down))
    chunks = []
    for part, sums in enumerate((early, late)):
        kept = (hidden0, hidden1)[part]
        (chunk,) = act(2, part, at, sums, stats0, gain_rows[part], saved0[part], kept)
        chunks.append(chunk)
    parts = along_tp(row_out(2, at, *swapped(chunks), (gain, feeds, up, down)))
    base = jnp.where(is_first, back, middle)
    return along_tp(finish(parts, base, True)).reshape(section_feeds.shape)


def solution(mesh):
    placed = (
        P("section", None, None, "row"),
        P("section", "row"),
        P("section", "row", "tp"),
        P("section", "tp", "row"),
    )
    return jax.shard_map(
        body, mesh=mesh, in_specs=placed, out_specs=P("section", None, None, "row"), check_vma=False
    )
```

```python
import functools

import jax
import jax.numpy as jnp
from jax import lax
from jax.experimental import pallas as pl
from jax.experimental.pallas import tpu as pltpu
from jax.sharding import PartitionSpec as P

epsilon = 1e-05
gelu_coeff = 0.7978845608028654
LANES = 128
EXTRA = 32
f32 = jnp.float32
bf16 = jnp.bfloat16
NN = (((1,), (0,)), ((), ()))
NT = (((1,), (1,)), ((), ()))
HBM = pl.BlockSpec(memory_space=pltpu.HBM)
VMEM = pl.BlockSpec(memory_space=pltpu.VMEM)
SMEM = pl.BlockSpec(memory_space=pltpu.SMEM)


def gelu_gate(inputs, square):
    inner = inputs * (gelu_coeff + gelu_coeff * 0.044715 * square)
    return 0.5 + 0.5 * jnp.tanh(inner)


def gelu_slope(inputs, square, gate):
    rise = inputs * (2.0 * gelu_coeff + 6.0 * gelu_coeff * 0.044715 * square)
    return gate * (1.0 + (1.0 - gate) * rise)


def pieces(value):
    high = value.astype(bf16)
    rest = value - high.astype(f32)
    middle = rest.astype(bf16)
    low = (rest - middle.astype(f32)).astype(bf16)
    return high, middle, low


def pieces32(value):
    return tuple(part.astype(f32) for part in pieces(value))


def mul(a, b, dims):
    return lax.dot_general(a, b, dims, preferred_element_type=f32)


def norm_stats(raw, gain_row):
    values = raw.astype(f32)
    mean = jnp.sum(values, axis=1, keepdims=True) / values.shape[1]
    centred = values - mean
    squares = jnp.sum(centred * centred, axis=1, keepdims=True)
    return (centred * gain_row).astype(bf16), pieces32(mean) + pieces32(squares)


def put_stats(to, start, lanes, stats, row_at):
    lane = lax.broadcasted_iota(jnp.int32, (1, LANES), 1)
    ext = jnp.zeros((stats[0].shape[0], LANES), f32)
    for i, part in enumerate(stats):
        ext = ext + jnp.where(lane == i * 8 + row_at, part, 0.0)
    to[pl.ds(start, ext.shape[0]), pl.ds(lanes, LANES)] = ext.astype(to.dtype)


def placed(parts, row_at):
    spot = lax.broadcasted_iota(jnp.int32, (EXTRA, 1), 0)
    return sum(jnp.where(spot == 3 * row_at + j, part, 0.0) for j, part in enumerate(parts))


def store_halves(own, other, columns, result):
    half = result.shape[0] // 2
    own[pl.ds(0, half), columns] = result[:half]
    other[pl.ds(0, half), columns] = result[half:].astype(bf16)


def start_kernel(at, x, gain, up, down, *refs):
    outs, (xs, x_here, gain_here, up_tiles, down_tiles, sems) = refs[:4], refs[4:]
    first = at[0] == 1
    core, row_at = at[1], at[2]
    count, _, wide = up_tiles.shape
    half = outs[0].shape[0] - EXTRA
    columns = outs[2].shape[1]

    def up_copy(n):
        return pltpu.make_async_copy(up.at[:, pl.ds(n * wide, wide)], up_tiles.at[n], sems.at[0, n])

    def down_copy(n):
        return pltpu.make_async_copy(down.at[pl.ds(n * wide, wide)], down_tiles.at[n], sems.at[1, n])

    x_copy = pltpu.make_async_copy(x, x_here, sems.at[2, 0])
    gain_copy = pltpu.make_async_copy(gain, gain_here, sems.at[2, 1])
    x_copy.start()
    gain_copy.start()

    @pl.when(jnp.logical_not(first))
    def _():
        for n in range(count):
            down_copy(n).start()

    for n in range(count):
        up_copy(n).start()
    x_copy.wait()
    gain_copy.wait()
    gain_row = gain_here[...]
    for kk in range(2):

        def prepare(p, carry):
            raw = x_here[(core + kk) % 2, p]
            scaled, stats = norm_stats(raw, gain_row)
            rows = pl.ds(pl.multiple_of((kk * 4 + p) * 32, 32), 32)
            xs[rows, :] = jnp.where(first, scaled, raw)
            put_stats(outs[kk], pl.multiple_of(p * 32, 32), columns, stats, row_at)
            return carry

        lax.fori_loop(0, 4, prepare, 0)
    xs[pl.ds(2 * half, EXTRA), :] = placed(pieces32(gain_row), row_at).astype(bf16)
    for to in outs[:2]:
        to[pl.ds(half, EXTRA), pl.ds(columns, LANES)] = jnp.zeros((EXTRA, LANES), to.dtype)

    for n in range(count):
        own, other = outs[n // 2 * 2 : n // 2 * 2 + 2]
        columns_at = pl.ds(n % 2 * wide, wide)

        def store(result, extra):
            store_halves(own, other, columns_at, result)
            rows = placed(pieces32(jnp.sum(extra, axis=0, keepdims=True)), row_at)
            own[pl.ds(half, EXTRA), columns_at] = rows
            other[pl.ds(half, EXTRA), columns_at] = rows.astype(bf16)

        @pl.when(first)
        def _():
            up_copy(n).wait()
            result = mul(xs[...], up_tiles[n], NN)
            store(result[: 2 * half], result[2 * half :])

        @pl.when(jnp.logical_not(first))
        def _():
            down_copy(n).wait()
            result = mul(xs[pl.ds(0, 2 * half), :], down_tiles[n], NT)
            up_copy(n).wait()
            store(result, mul(xs[pl.ds(2 * half, EXTRA), :], up_tiles[n], NN))


def start_in(at, x, gain, up, down):
    width, hidden = up.shape
    wide, count = hidden // 4, 4
    rows = 128 + EXTRA
    outs = pl.pallas_call(
        start_kernel,
        out_shape=half_shapes(rows, hidden // 2 + LANES) + half_shapes(rows, hidden // 2),
        in_specs=[SMEM] + [HBM] * 4,
        out_specs=[VMEM] * 4,
        scratch_shapes=[
            pltpu.VMEM((256 + EXTRA, width), bf16),
            pltpu.VMEM(x.shape, bf16),
            pltpu.VMEM(gain.shape, f32),
            pltpu.VMEM((count, width, wide), bf16),
            pltpu.VMEM((count, wide, width), bf16),
            pltpu.SemaphoreType.DMA((3, count)),
        ],
        compiler_params=pltpu.CompilerParams(vmem_limit_bytes=24 * 1024 * 1024),
        cost_estimate=pl.CostEstimate(
            flops=2 * 256 * width * hidden, bytes_accessed=2 * width * hidden, transcendentals=0
        ),
        name="start_in",
    )(at, *(pltpu.with_memory_space_constraint(v, pltpu.HBM) for v in (x, gain, up, down)))
    return outs[:2], outs[2:]


def up_kernel(at, x, gain, up, *refs):
    outs, (xs, up_tiles, sems) = refs[:4], refs[4:]
    count, _, wide = up_tiles.shape
    columns = outs[2].shape[1]

    def up_copy(n):
        return pltpu.make_async_copy(up.at[:, pl.ds(n * wide, wide)], up_tiles.at[n], sems.at[n])

    for n in range(count):
        up_copy(n).start()
    gain_row = gain[...]
    for kk in range(2):

        def prepare(p, carry):
            scaled, stats = norm_stats(x[(at[1] + kk) % 2 * 4 + p], gain_row)
            xs[pl.ds(pl.multiple_of((kk * 4 + p) * 32, 32), 32), :] = scaled
            put_stats(outs[kk], pl.multiple_of(p * 32, 32), columns, stats, at[2])
            return carry

        lax.fori_loop(0, 4, prepare, 0)
    for n in range(count):
        up_copy(n).wait()
        result = mul(xs[...], up_tiles[n], NN)
        store_halves(*outs[n // 2 * 2 : n // 2 * 2 + 2], pl.ds(n % 2 * wide, wide), result)


def up_in(at, x, gain, up):
    width, hidden = up.shape
    wide, count = hidden // 4, 4
    outs = pl.pallas_call(
        up_kernel,
        out_shape=half_shapes(128, hidden // 2 + LANES) + half_shapes(128, hidden // 2),
        in_specs=[SMEM, VMEM, VMEM, HBM],
        out_specs=[VMEM] * 4,
        scratch_shapes=[
            pltpu.VMEM((256, width), bf16),
            pltpu.VMEM((count, width, wide), bf16),
            pltpu.SemaphoreType.DMA((count,)),
        ],
        compiler_params=pltpu.CompilerParams(vmem_limit_bytes=14 * 1024 * 1024),
        cost_estimate=pl.CostEstimate(
            flops=2 * 256 * width * hidden, bytes_accessed=2 * width * hidden, transcendentals=0
        ),
        name="up_in",
    )(at, x, gain, pltpu.with_memory_space_constraint(up, pltpu.HBM))
    return outs[:2], outs[2:]


def down_back_kernel(part, at, x, down, own, other):
    wide = own.shape[1] // 2
    half = own.shape[0]
    for n in range(2):
        result = mul(x[...], down[pl.ds((2 * part + n) * wide, wide), :], NT)
        low, high = result[:half], result[half:]
        columns = pl.ds(n * wide, wide)
        own[:, columns] = jnp.where(at[1] == 0, low, high)
        other[:, columns] = jnp.where(at[1] == 0, high, low).astype(bf16)


def local_call(kernel, shapes, operands, name, flops, nbytes, smem=False, scratch=()):
    specs = [SMEM if smem and i == 0 else VMEM for i in range(len(operands))]
    return pl.pallas_call(
        kernel,
        out_shape=shapes,
        in_specs=specs,
        out_specs=[VMEM] * len(shapes),
        scratch_shapes=list(scratch),
        compiler_params=pltpu.CompilerParams(vmem_limit_bytes=6 * 1024 * 1024),
        cost_estimate=pl.CostEstimate(flops=flops, bytes_accessed=nbytes, transcendentals=0),
        name=name,
    )(*operands)


def half_shapes(rows, columns):
    return [
        jax.ShapeDtypeStruct((rows, columns), f32),
        jax.ShapeDtypeStruct((rows, columns), bf16),
    ]


def down_back_in(at, x, down):
    hidden, width = down.shape
    return [
        local_call(
            functools.partial(down_back_kernel, part),
            half_shapes(128, hidden // 2),
            (at, x.reshape(256, width), down),
            f"down_back_{part}",
            256 * width * hidden,
            width * hidden,
            smem=True,
        )
        for part in range(2)
    ]


def row_out_kernel(mode, at, *refs):
    inputs, rest, (out, xs) = refs[:4], refs[4:-2], refs[-2:]
    first = at[0] == 1
    half, columns = 128, xs.shape[1] // 2
    width = out.shape[-1]
    if mode:
        for i in range(2):
            for j in range(2):
                ref = inputs[2 * i + j]
                xs[pl.ds(i * half, half), pl.ds(j * columns, columns)] = ref[:, pl.ds(0, columns)]

    def direct(weight):
        def step(n, carry):
            at_n = pl.ds(pl.multiple_of(n * 512, 512), 512)
            for i in range(2):
                result = mul(inputs[2 * i][...], weight[pl.ds(0, columns), at_n], NN)
                result = result + mul(inputs[2 * i + 1][...], weight[pl.ds(columns, columns), at_n], NN)
                for k in range(4):
                    out[(4 * i + k + 4 * at[1]) % 8, :, at_n] = result[k * 32 : k * 32 + 32].astype(bf16)
            return carry

        lax.fori_loop(0, width // 512, step, 0)

    def terms():
        gain, x = rest[:2]
        for i in range(2):
            early, late = (r[:, pl.ds(columns, LANES)].astype(f32) for r in inputs[2 * i : 2 * i + 2])
            ext = early + late
            first0, second0, first1, second1, mean, inv_std = (
                ext[:, 3 * k : 3 * k + 1] + ext[:, 3 * k + 1 : 3 * k + 2] + ext[:, 3 * k + 2 : 3 * k + 3]
                for k in range(6)
            )
            for p in range(4):
                pick = slice(p * 32, p * 32 + 32)
                yield (
                    i * 4 + p,
                    gain,
                    x.at[(at[1] + i) % 2, p] if mode == 2 else x.at[(at[1] + i) % 2 * 4 + p],
                    (first0 + first1)[pick],
                    (second0 + second1)[pick],
                    mean[pick],
                    inv_std[pick],
                )

    def steps(weight, dims, back):
        saved = list(terms()) if back else []

        def step(n, carry):
            at_n = pl.ds(pl.multiple_of(n * 512, 512), 512)
            tile = weight[:, at_n] if dims is NN else weight[at_n, :]
            result = mul(xs[...], tile, dims)
            if not back:
                for k in range(8):
                    out[(k + 4 * at[1]) % 8, :, at_n] = result[k * 32 : k * 32 + 32].astype(bf16)
            for k, gain, x, first_sum, second_sum, mean, inv_std in saved:
                grad = result[k * 32 : k * 32 + 32] * gain[:, at_n]
                normed = (x[:, at_n].astype(f32) - mean) * inv_std
                out[(k + 4 * at[1]) % 8, :, at_n] = (inv_std * (grad - first_sum - normed * second_sum)).astype(bf16)
            return carry

        lax.fori_loop(0, width // 512, step, 0)

    if mode == 0:
        pl.when(first)(lambda: direct(rest[0]))
    elif mode == 1:
        steps(rest[2], NT, True)
    else:
        pl.when(first)(lambda: steps(rest[2], NT, True))
        pl.when(jnp.logical_not(first))(lambda: steps(rest[3], NN, False))


def row_out(mode, at, mine, others, rest):
    hidden, width = max(rest[-1].shape), min(rest[-1].shape)
    (out,) = local_call(
        functools.partial(row_out_kernel, mode),
        [jax.ShapeDtypeStruct((8, 32, width), bf16)],
        (at, *mine, *others, *rest),
        f"row_out_{mode}",
        2 * 256 * width * hidden,
        2 * width * hidden,
        smem=True,
        scratch=[pltpu.VMEM((256, hidden), bf16)],
    )
    return out


MEAN, INV = 0, 1
COMBOS = ((0, 0), (0, 1), (1, 0), (0, 2), (1, 1), (2, 0))


def act_kernel(mode, part, at, *refs):
    refs = list(refs)
    first = at[0] == 1
    sums = [(refs.pop(0), refs.pop(0)) for _ in range(2)]
    stats = refs.pop(0) if mode == 2 or part else None
    factors = refs.pop(0) if mode != 2 and part else None
    gains = refs.pop(0) if mode == 1 else None
    totals = refs.pop(0) if mode else None
    saved = refs.pop(0) if mode else None
    hidden = refs.pop(0) if mode == 2 else None
    chunk = refs.pop(0)
    saved_out = refs.pop(0) if mode == 0 else None
    gains_out = refs.pop(0) if mode == 0 else None
    totals_out = refs.pop(0) if mode == 0 else None
    hidden_out = refs.pop(0) if mode == 1 else None
    stats_out = refs.pop(0) if mode != 2 and part == 0 else None
    factors_out = refs.pop(0) if mode != 2 and part == 0 else None
    shifted = refs.pop(0) if mode != 2 else None
    wide = 1024
    total_width = 8192
    lane = lax.broadcasted_iota(jnp.int32, (1, LANES), 1)
    if mode == 0:
        for q, (held, arrived) in enumerate(sums):
            columns = pl.ds(q * wide, wide)
            extra = held[pl.ds(128, EXTRA), pl.ds(0, wide)] + arrived[pl.ds(128, EXTRA), pl.ds(0, wide)].astype(f32)
            rows8 = jnp.concatenate(
                [jnp.sum(extra[3 * r : 3 * r + 3], axis=0, keepdims=True) for r in range(8)], axis=0
            )
            gains_out[:, columns] = rows8
            totals_out[:, columns] = jnp.sum(rows8, axis=0, keepdims=True)
        gains = gains_out
    if stats_out is not None:
        stats = stats_out
        held, arrived = sums[1]
        ext = held[pl.ds(0, 128), pl.ds(wide, LANES)] + arrived[pl.ds(0, 128), pl.ds(wide, LANES)].astype(f32)
        means = [sum(ext[:, 8 * k + r : 8 * k + r + 1] for k in range(3)) for r in range(8)]
        mean = sum(means) / 8
        shifts = [value - mean for value in means]
        squares = jnp.sum(jnp.where((lane >= 24) & (lane < 48), ext, 0.0), axis=1, keepdims=True)
        variance = (squares + wide * sum(value * value for value in shifts)) / total_width
        inv_std = lax.rsqrt(variance + epsilon)
        if mode == 0:
            inv_std = jnp.where(first, inv_std, 1.0)
            shifts = [jnp.where(first, value, 0.0) for value in shifts]
        out = jnp.where(lane == MEAN, mean, 0.0) + jnp.where(lane == INV, inv_std, 0.0)
        stats[...] = out
        placed_at = jnp.zeros((128, LANES), f32)
        for r, value in enumerate(shifts):
            split = pieces32(value)
            for k, (j, _) in enumerate(COMBOS):
                placed_at = placed_at + jnp.where(lane == 8 * k + r, split[j], 0.0)
        factors_out[...] = placed_at.astype(bf16)
        factors = factors_out
    if mode != 2:
        for q in range(4):
            columns = pl.ds(q * 512, 512)
            split = pieces32(gains[:, columns])
            zeros = jnp.zeros((LANES - 8 * len(COMBOS), 512), f32)
            stacked = jnp.concatenate([split[j] for _, j in COMBOS] + [zeros], axis=0)
            shifted[:, columns] = mul(factors[...], stacked.astype(bf16), NN)

    size, span = 32, 256

    def block(i, carry):
        rows = pl.ds(pl.multiple_of(i * size, size), size)
        here = stats[rows, :]
        mean, inv_std = here[:, MEAN : MEAN + 1], here[:, INV : INV + 1]
        firsts = jnp.zeros((size, span), f32)
        seconds = jnp.zeros((size, span), f32)
        for n in range(2 * wide // span):
            columns = pl.ds(n * span, span)
            held, arrived = sums[n * span // wide]
            inner = pl.ds(n * span % wide, span)
            value = held[rows, inner] + arrived[rows, inner].astype(f32)
            if mode != 2:
                value = inv_std * (value + shifted[rows, columns])
            pre = saved[rows, columns] if mode == 2 else value
            square = pre * pre
            gate = gelu_gate(pre, square)
            if mode == 0:
                saved_out[rows, columns] = pre
                chunk[rows, columns] = (pre * gate).astype(bf16)
                continue
            slope = gelu_slope(pre, square, gate)
            grad = (value if mode == 2 else saved[rows, columns]) * slope
            grad_sent = grad.astype(bf16)
            if mode == 1:
                hidden_out[rows, columns] = (pre * gate).astype(bf16)
                chunk[rows, columns] = grad_sent
            else:
                chunk[rows, columns] = jnp.where(first, grad_sent, hidden[rows, columns])
            grad = grad_sent.astype(f32)
            firsts = firsts + grad * totals[:, columns]
            seconds = seconds + grad * pre
        if mode:
            values = [
                jnp.sum(v, axis=1, keepdims=True) / total_width for v in (firsts, seconds)
            ] + ([mean, inv_std] if part else [])
            ext = jnp.zeros((size, LANES), f32)
            spot = 6 * part
            for value in values:
                for piece in pieces32(value):
                    ext = ext + jnp.where(lane == spot, piece, 0.0)
                    spot += 1
            chunk[rows, pl.ds(2 * wide, LANES)] = ext.astype(bf16)
        return carry

    lax.fori_loop(0, 128 // size, block, 0)


def act(mode, part, at, sums, stats, gains, saved, hidden):
    wide = 2048
    operands = [at] + [ref for pair in sums for ref in pair]
    if mode == 2 or part:
        operands.append(stats[0])
    if mode != 2 and part:
        operands.append(stats[1])
    if mode == 1:
        operands.append(gains[0])
    if mode:
        operands += [gains[1], saved]
    if mode == 2:
        operands.append(hidden)
    shapes = [jax.ShapeDtypeStruct((128, wide + (LANES if mode else 0)), bf16)]
    if mode == 0:
        shapes.append(jax.ShapeDtypeStruct((128, wide), f32))
        shapes.append(jax.ShapeDtypeStruct((8, wide), f32))
        shapes.append(jax.ShapeDtypeStruct((1, wide), f32))
    if mode == 1:
        shapes.append(jax.ShapeDtypeStruct((128, wide), bf16))
    if mode != 2 and part == 0:
        shapes.append(jax.ShapeDtypeStruct((128, LANES), f32))
        shapes.append(jax.ShapeDtypeStruct((128, LANES), bf16))
    return local_call(
        functools.partial(act_kernel, mode, part),
        shapes,
        operands,
        f"act_{mode}_{part}",
        40 * 128 * wide,
        16 * 128 * wide,
        smem=True,
        scratch=[pltpu.VMEM((128, wide), f32)] if mode != 2 else (),
    )


def finish_kernel(parts, base, out):
    total = base[...].astype(f32)
    for k in range(8):
        total = total + parts[k].astype(f32)
    total = total.astype(bf16)
    if len(out.shape) == 2:
        out[...] = total
    else:
        for k in range(8):
            out[k] = total


def finish(parts, base, copies):
    block, width = base.shape
    (out,) = local_call(
        finish_kernel,
        [jax.ShapeDtypeStruct((8, block, width) if copies else base.shape, bf16)],
        (parts, base),
        "finish",
        8 * block * width,
        20 * block * width,
    )
    return out


def permuted(array, axis, mapping):
    return lax.ppermute(array, axis, [(i, mapping(i)) for i in range(lax.axis_size(axis))])


def body(section_feeds, norm_gain, up_weight, down_weight):
    up = up_weight[0]
    down = down_weight[0]
    gain = norm_gain
    width, hidden = up.shape
    micro, rows = section_feeds.shape[1], section_feeds.shape[2]
    rsize, tsize = lax.axis_size("row"), lax.axis_size("tp")
    tokens = micro * rows
    block = tokens // tsize
    is_first = lax.axis_index("section") == 0
    row_at = lax.axis_index("row")
    tp_at = lax.axis_index("tp")
    core = row_at % 2
    at = jnp.stack([is_first.astype(jnp.int32), core, row_at])

    def pair(i):
        return i ^ 1

    def near(i):
        return i ^ 2

    def far(i):
        return i ^ 6

    def row_sum(halves):
        sums = []
        for own, other in halves:
            arrived = permuted(other, "row", pair)
            for columns in (slice(0, hidden // 4), slice(hidden // 4, None)):
                sums.append(own[:, columns] + arrived[:, columns].astype(f32))
        ways = (near, far, near, far)
        arrived = [permuted(h.astype(bf16), "row", way) for h, way in zip(sums, ways)]
        sums = [h + r.astype(f32) for h, r in zip(sums, arrived)]
        ways = (far, near, far, near)
        arrived = [permuted(h.astype(bf16), "row", way) for h, way in zip(sums, ways)]
        quarters = list(zip(sums, arrived))
        return quarters[:2], quarters[2:]

    def swapped(chunks):
        return chunks, [permuted(chunk, "row", pair) for chunk in chunks]

    def along_tp(part):
        return lax.all_to_all(part, "tp", 0, 0)

    blocks = rows // block
    feeds = section_feeds[0].reshape(micro, blocks, block, width)
    own_feed = lax.dynamic_index_in_dim(
        feeds.reshape(tsize, block, width), tp_at, 0, keepdims=False
    )
    early, late = row_sum(start_in(at, feeds, gain, up, down))
    chunk0, saved00, *gains0, stats, factors = act(0, 0, at, early, None, None, None, None)
    stats0 = (stats, factors)
    chunk1, saved01, *gains1 = act(0, 1, at, late, stats0, None, None, None)
    chunks, saved0, gain_rows = [chunk0, chunk1], [saved00, saved01], [gains0, gains1]
    parts = along_tp(row_out(0, at, *swapped(chunks), (down,)))
    middle = lax.ppermute(finish(parts, own_feed, False), "section", [(0, 1)])
    middles = along_tp(jnp.broadcast_to(middle[None], (tsize,) + middle.shape))

    early, late = row_sum(up_in(at, middles, gain, up))
    chunk0, hidden0, *stats1 = act(1, 0, at, early, None, gain_rows[0], saved0[0], None)
    chunk1, hidden1 = act(1, 1, at, late, stats1, gain_rows[1], saved0[1], None)
    chunks = [chunk0, chunk1]
    parts = along_tp(row_out(1, at, *swapped(chunks), (gain, middles, up)))
    back = lax.ppermute(finish(parts, own_feed, False), "section", [(1, 0)])
    backs = along_tp(jnp.broadcast_to(back[None], (tsize,) + back.shape))

    early, late = row_sum(down_back_in(at, backs, down))
    chunks = []
    for part, sums in enumerate((early, late)):
        kept = (hidden0, hidden1)[part]
        (chunk,) = act(2, part, at, sums, stats0, gain_rows[part], saved0[part], kept)
        chunks.append(chunk)
    parts = along_tp(row_out(2, at, *swapped(chunks), (gain, feeds, up, down)))
    base = jnp.where(is_first, back, middle)
    return along_tp(finish(parts, base, True)).reshape(section_feeds.shape)


def solution(mesh):
    placed = (
        P("section", None, None, "row"),
        P("section", "row"),
        P("section", "row", "tp"),
        P("section", "tp", "row"),
    )
    return jax.shard_map(
        body, mesh=mesh, in_specs=placed, out_specs=P("section", None, None, "row"), check_vma=False
    )
```
